256 devices in a mesh: head: 8 (over x, core), ctx: 32 (over y, z).
Axes of the slice: x: 4, y: 4, z: 8, core: 2. Of those that a mesh axis runs over, the one named last changes fastest.
Arguments:
- queries: bfloat16 [32768, 4096], P('ctx', 'head'), may hold values from -108 to 108
- key_states: bfloat16 [32768, 1024], P(('ctx', 'head')), may hold values from -9 to 9
- value_states: bfloat16 [32768, 1024], P(('ctx', 'head')), may hold values from -6 to 6
- block_lists: int32 [512, 8], P('ctx'), may hold values from 0 to 511, as said below
- out_grad: bfloat16 [32768, 4096], P('ctx', 'head'), may hold values from -12 to 12
Outputs:
- attended: bfloat16 [32768, 4096], P('ctx', 'head')
- query_grad: bfloat16 [32768, 4096], P('ctx', 'head')
- key_grad: bfloat16 [32768, 1024], P(('ctx', 'head'))
- value_grad: bfloat16 [32768, 1024], P(('ctx', 'head'))
The draws below stay inside these ranges and needn't reach their ends.
Inputs may be any that keep to these rules, and one draw needn't show every extreme that they name: `block_lists`: row i's first entry is i and every entry is at most i (repeats allowed). The lists of the 16 query blocks of one ctx index c name at most 3 distinct blocks held by any other ctx index (index c holds blocks c * 16 to c * 16 + 15).
All inputs are finite; a program needn't handle non-finite values.
Results may differ from the reference program's by a relative error of at most 0.04.
Values may be sent and summed in bfloat16 or wider, within the bound.
A program may use at most 128 MiB of HBM per device.

```python
import jax
import jax.numpy as jnp
from jax import lax

HEADS = 32
KV_HEADS = 8
HEAD_DIM = 128
GROUP = 4
BLK = 64
LIST = 8
CAP = 3
QB_DEV = 16
SEQ = 32768
NBLOCKS = 512


def shared_keys(key):
    base = 1.5 * jax.random.normal(jax.random.fold_in(key, 7), (SEQ, KV_HEADS * HEAD_DIM), jnp.float32)
    base = jnp.clip(base, -9.0, 9.0)
    return base


def draw_key_states(key, part):
    return shared_keys(key).astype(jnp.bfloat16)


def draw_queries(key, part):
    drawn = jnp.clip(1.5 * jax.random.normal(jax.random.fold_in(key, 9), (SEQ, HEADS * HEAD_DIM), jnp.float32), -9.0, 9.0)
    return drawn.astype(jnp.bfloat16)


def draw_block_lists(key, part):
    shard_count = NBLOCKS // QB_DEV
    slots = QB_DEV * (LIST - 1)
    pool_size = shard_count * CAP
    keys_all = jax.random.split(key, 6)
    picks = jax.random.randint(keys_all[0], (shard_count, shard_count, QB_DEV), 0, 1 << 20) * QB_DEV + jnp.arange(QB_DEV)
    chosen = jnp.argsort(picks, axis=2)[:, :, :CAP]
    owners = jnp.arange(shard_count)
    pool = (owners[None, :, None] * QB_DEV + chosen).reshape(shard_count, pool_size)
    valid = jnp.broadcast_to(owners[None, :, None] < owners[:, None, None], (shard_count, shard_count, CAP)).reshape(shard_count, pool_size)
    order_score = jnp.where(valid, jax.random.randint(keys_all[1], (shard_count, pool_size), 0, 1 << 20), 1 << 21)
    order_score = order_score * pool_size + jnp.arange(pool_size)
    pool_sorted = jnp.take_along_axis(pool, jnp.argsort(order_score, axis=1), axis=1)
    count = CAP * owners
    slot_ids = jnp.arange(slots)
    random_pick = jax.random.randint(keys_all[2], (shard_count, slots), 0, 1 << 20) % jnp.maximum(count, 1)[:, None]
    pool_index = jnp.where(slot_ids[None, :] < count[:, None], slot_ids[None, :], random_pick)
    remote_blocks = jnp.take_along_axis(pool_sorted, pool_index, axis=1)
    shuffle_score = jax.random.randint(keys_all[3], (shard_count, slots), 0, 1 << 20) * slots + slot_ids
    shuffle = jnp.argsort(shuffle_score, axis=1)
    remote_blocks = jnp.take_along_axis(remote_blocks, shuffle, axis=1)
    covering = jnp.take_along_axis(jnp.broadcast_to(slot_ids[None, :] < count[:, None], (shard_count, slots)), shuffle, axis=1)
    coin = jax.random.randint(keys_all[4], (shard_count, slots), 0, 2) == 0
    use_remote = (count[:, None] > 0) & (covering | coin)
    local_block = jnp.broadcast_to(slot_ids[None, :] // (LIST - 1), (shard_count, slots))
    local_pick = jax.random.randint(keys_all[5], (shard_count, slots), 0, local_block + 1)
    local_ids = owners[:, None] * QB_DEV + local_pick
    others = jnp.where(use_remote, remote_blocks, local_ids).reshape(NBLOCKS, LIST - 1)
    return jnp.concatenate([jnp.arange(NBLOCKS)[:, None], others], axis=1).astype(jnp.int32)


def steps_of(key, shape, cuts, smallest, top_value):
    factor_of, own = 1.0, jax.random.fold_in(key, 6)
    for axis_at, parts in cuts:
        steps = jnp.exp(jax.random.uniform(jax.random.fold_in(own, axis_at), (parts,), jnp.float32, smallest / len(cuts), top_value / len(cuts)))
        factor_of = factor_of * jnp.repeat(steps, shape[axis_at] // parts).reshape([-1 if axis == axis_at else 1 for axis in range(len(shape))])
    return factor_of


def scatter_about(rng, extent, scale, limit, pieces=(), held_as=jnp.bfloat16):
    factor_of = steps_of(rng, extent, pieces, -0.22, 0.18) if pieces else 1.0
    result = jax.random.normal(rng, extent, jnp.float32) * scale * factor_of
    return jnp.minimum(jnp.maximum(result, -limit), limit).astype(held_as)


def setup_inputs(seed: int = 0) -> dict:
    keys = jax.random.split(jax.random.key(seed), 6)
    return {
        "queries": draw_queries(jax.random.fold_in(keys[5], 71), 0),
        "key_states": draw_key_states(jax.random.fold_in(keys[5], 71), 0),
        "value_states": scatter_about(keys[2], (SEQ, KV_HEADS * HEAD_DIM), 1.0, 6.0, ((0, 256),)),
        "block_lists": draw_block_lists(jax.random.fold_in(keys[5], 71), 0),
        "out_grad": scatter_about(keys[4], (SEQ, HEADS * HEAD_DIM), 2.0, 12.0, ((0, 32), (1, 8))),
    }


NEG_FILL = -1.0e30


def round_bf16(values):
    return lax.optimization_barrier(values.astype(jnp.bfloat16)).astype(jnp.float32)


def reference(queries, key_states, value_states, block_lists, out_grad):
    softmax_scale = HEAD_DIM ** -0.5
    query_blocks = queries.astype(jnp.float32).reshape(NBLOCKS, BLK, KV_HEADS, GROUP, HEAD_DIM)
    grad_blocks = out_grad.astype(jnp.float32).reshape(NBLOCKS, BLK, KV_HEADS, GROUP, HEAD_DIM)
    key_blocks = key_states.astype(jnp.float32).reshape(NBLOCKS, BLK, KV_HEADS, HEAD_DIM)
    value_blocks = value_states.astype(jnp.float32).reshape(NBLOCKS, BLK, KV_HEADS, HEAD_DIM)
    offsets = jnp.arange(BLK, dtype=jnp.int32)

    def visit(carry, index):
        key_acc, value_acc = carry
        listed = block_lists[index]
        key_rows = key_blocks[listed].reshape(LIST * BLK, KV_HEADS, HEAD_DIM)
        value_rows = value_blocks[listed].reshape(LIST * BLK, KV_HEADS, HEAD_DIM)
        query_rows = query_blocks[index]
        grad_rows = grad_blocks[index]
        scores = jnp.einsum('tkgd,skd->kgts', query_rows, key_rows) * softmax_scale
        key_pos = (listed[:, None] * BLK + offsets[None, :]).reshape(-1)
        query_pos = index * BLK + offsets
        visible = key_pos[None, :] <= query_pos[:, None]
        scores = jnp.where(visible, scores, NEG_FILL)
        row_peak = jnp.max(scores, axis=-1, keepdims=True)
        expo = jnp.exp(scores - row_peak)
        attn_probs = expo / jnp.sum(expo, axis=-1, keepdims=True)
        probs_low = round_bf16(attn_probs)
        attended = round_bf16(jnp.einsum('kgts,skd->tkgd', probs_low, value_rows))
        row_delta = jnp.transpose(jnp.sum(grad_rows * attended, axis=-1), (1, 2, 0))[..., None]
        dprob = jnp.einsum('tkgd,skd->kgts', grad_rows, value_rows)
        dscore = round_bf16(attn_probs * (dprob - row_delta))
        query_part = jnp.einsum('kgts,skd->tkgd', dscore, key_rows) * softmax_scale
        key_part = jnp.einsum('kgts,tkgd->skd', dscore, query_rows) * softmax_scale
        value_part = jnp.einsum('kgts,tkgd->skd', probs_low, grad_rows)
        key_acc = key_acc.at[listed].add(key_part.reshape(LIST, BLK, KV_HEADS, HEAD_DIM))
        value_acc = value_acc.at[listed].add(value_part.reshape(LIST, BLK, KV_HEADS, HEAD_DIM))
        return (key_acc, value_acc), (attended.astype(jnp.bfloat16), query_part.astype(jnp.bfloat16))

    zeros = jnp.zeros((NBLOCKS, BLK, KV_HEADS, HEAD_DIM), jnp.float32)
    (key_acc, value_acc), (attended, query_grad) = lax.scan(visit, (zeros, zeros), jnp.arange(NBLOCKS, dtype=jnp.int32))
    return (attended.reshape(SEQ, HEADS * HEAD_DIM),
            query_grad.reshape(SEQ, HEADS * HEAD_DIM),
            key_acc.reshape(SEQ, KV_HEADS * HEAD_DIM).astype(jnp.bfloat16),
            value_acc.reshape(SEQ, KV_HEADS * HEAD_DIM).astype(jnp.bfloat16))
```

```python
import functools

import jax
import jax.numpy as jnp
from jax import lax
from jax.experimental import pallas as pl
from jax.experimental.pallas import tpu as pltpu
from jax.sharding import PartitionSpec as P

HEAD_DIM = 128
GROUP = 4
BLK = 64
LIST = 8
CAP = 3
QB = 16
ROWS = 4
COLS = 8
CTX = ROWS * COLS
HEADS_AX = 8
TOK = QB * BLK
SLOT = CAP * BLK
REM = CTX * SLOT
ALL = TOK + REM
NEG_FILL = -1e30
SCALE = HEAD_DIM ** (-0.5)
LOG2E = 1.4426950408889634
STEP_BLOCKS = 2

NT = (((1,), (1,)), ((), ()))
TN = (((0,), (0,)), ((), ()))
NN = (((1,), (0,)), ((), ()))


def dot(a, b, dims):
    return lax.dot_general(a, b, dims, preferred_element_type=jnp.float32)


def attend_kernel(
    lists, q_ref, do_ref, kloc, vloc, krem, vrem,
    att_ref, dq_ref, gkl, gvl, gkr, gvr,
    kall, vall, gk, gv, masks, sems,
):
    step = pl.program_id(0)
    me = lax.axis_index("ctx")

    @pl.when(step == 0)
    def _():
        copies = [
            pltpu.make_async_copy(kloc, kall.at[pl.ds(0, TOK)], sems.at[0]),
            pltpu.make_async_copy(krem, kall.at[pl.ds(TOK, REM)], sems.at[1]),
            pltpu.make_async_copy(vloc, vall.at[pl.ds(0, TOK)], sems.at[2]),
            pltpu.make_async_copy(vrem, vall.at[pl.ds(TOK, REM)], sems.at[3]),
        ]
        for copy in copies:
            copy.start()

        def clear(i, _):
            rows = pl.ds(pl.multiple_of(i * 256, 256), 256)
            gk[rows] = jnp.zeros((256, HEAD_DIM), jnp.float32)
            gv[rows] = jnp.zeros((256, HEAD_DIM), jnp.float32)
            return 0

        lax.fori_loop(0, ALL // 256, clear, 0)
        for owner in range(CTX):
            masks[owner] = 0
        for i in range(QB):
            for j in range(1, LIST):
                ref = lists[i, j]
                owner = lax.shift_right_logical(ref, 4)
                masks[owner] = masks[owner] | lax.shift_left(jnp.int32(1), ref & 15)
        for copy in copies:
            copy.wait()

    key_row = lax.broadcasted_iota(jnp.int32, (BLK, GROUP * BLK), 0)
    query_col = lax.broadcasted_iota(jnp.int32, (BLK, GROUP * BLK), 1) % BLK
    hidden = jnp.where(key_row > query_col, NEG_FILL, 0.0).astype(jnp.float32)

    for u in range(STEP_BLOCKS):
        i = step * STEP_BLOCKS + u
        rows = pl.ds(u * BLK, BLK)
        starts, flags = [], []
        for j in range(LIST):
            ref = lists[i, j]
            owner = lax.shift_right_logical(ref, 4)
            inner = ref & 15
            below = masks[owner] & (lax.shift_left(jnp.int32(1), inner) - 1)
            rank = (below != 0).astype(jnp.int32) + ((below & (below - 1)) != 0).astype(jnp.int32)
            slot = jnp.where(owner == me, inner, QB + owner * CAP + rank)
            starts.append(pl.multiple_of(slot * BLK, BLK))
            flags.append((ref == me * QB + i).astype(jnp.float32))
        q = jnp.concatenate(
            [q_ref[rows, pl.ds(g * HEAD_DIM, HEAD_DIM)] for g in range(GROUP)], axis=0
        )
        do = jnp.concatenate(
            [do_ref[rows, pl.ds(g * HEAD_DIM, HEAD_DIM)] for g in range(GROUP)], axis=0
        )
        keys = jnp.concatenate([kall[pl.ds(s, BLK)] for s in starts], axis=0)
        values = jnp.concatenate([vall[pl.ds(s, BLK)] for s in starts], axis=0)
        raw = dot(keys, q, NT) * (SCALE * LOG2E)
        parts = []
        for j in range(LIST):
            part = raw[j * BLK : (j + 1) * BLK]
            parts.append(part + (hidden if j == 0 else hidden * flags[j]))
        scores = jnp.concatenate(parts, axis=0)
        peak = jnp.max(scores, axis=0, keepdims=True)
        expo = jnp.exp2(scores - peak)
        probs = expo * (1.0 / jnp.sum(expo, axis=0, keepdims=True))
        probs_low = probs.astype(jnp.bfloat16)
        dprob = dot(values, do, NT)
        weighted = probs * dprob
        delta = jnp.sum(weighted, axis=0, keepdims=True)
        dscore = (weighted - probs * delta).astype(jnp.bfloat16)
        att = jnp.transpose(dot(values, probs_low, TN)).astype(jnp.bfloat16)
        dq = (jnp.transpose(dot(keys, dscore, TN)) * SCALE).astype(jnp.bfloat16)
        for g in range(GROUP):
            att_ref[rows, pl.ds(g * HEAD_DIM, HEAD_DIM)] = att[g * BLK : (g + 1) * BLK]
            dq_ref[rows, pl.ds(g * HEAD_DIM, HEAD_DIM)] = dq[g * BLK : (g + 1) * BLK]
        dv = dot(probs_low, do, NN)
        dk = dot(dscore, q, NN)
        for j in range(LIST):
            here = pl.ds(starts[j], BLK)
            gk[here] += dk[j * BLK : (j + 1) * BLK]
            gv[here] += dv[j * BLK : (j + 1) * BLK]

    @pl.when(step == QB // STEP_BLOCKS - 1)
    def _():
        gkl[...] = gk[pl.ds(0, TOK)] * SCALE
        gvl[...] = gv[pl.ds(0, TOK)]

        def put(o, _):
            src = pl.ds(pl.multiple_of(TOK + o * SLOT, BLK), SLOT)
            dst = pl.ds(pl.multiple_of(o * SLOT, BLK), SLOT)
            gkr[dst] = (gk[src] * SCALE).astype(jnp.bfloat16)
            gvr[dst] = gv[src].astype(jnp.bfloat16)
            return 0

        lax.fori_loop(0, me, put, 0)


def attend(lists, queries, out_grad, kloc, vloc, krem, vrem):
    bf16, f32 = jnp.bfloat16, jnp.float32
    wide = GROUP * HEAD_DIM
    tile = pl.BlockSpec((STEP_BLOCKS * BLK, wide), lambda s: (s, 0))
    whole = lambda n: pl.BlockSpec((n, HEAD_DIM), lambda s: (0, 0), pipeline_mode=pl.Buffered(1))
    anywhere = pl.BlockSpec(memory_space=pl.ANY)
    return pl.pallas_call(
        attend_kernel,
        grid=(QB // STEP_BLOCKS,),
        in_specs=[pl.BlockSpec(memory_space=pltpu.SMEM), tile, tile] + [anywhere] * 4,
        out_specs=[tile, tile, whole(TOK), whole(TOK), whole(REM), whole(REM)],
        out_shape=[
            jax.ShapeDtypeStruct((TOK, wide), bf16),
            jax.ShapeDtypeStruct((TOK, wide), bf16),
            jax.ShapeDtypeStruct((TOK, HEAD_DIM), f32),
            jax.ShapeDtypeStruct((TOK, HEAD_DIM), f32),
            jax.ShapeDtypeStruct((REM, HEAD_DIM), bf16),
            jax.ShapeDtypeStruct((REM, HEAD_DIM), bf16),
        ],
        scratch_shapes=[
            pltpu.VMEM((ALL, HEAD_DIM), bf16),
            pltpu.VMEM((ALL, HEAD_DIM), bf16),
            pltpu.VMEM((ALL, HEAD_DIM), f32),
            pltpu.VMEM((ALL, HEAD_DIM), f32),
            pltpu.SMEM((CTX,), jnp.int32),
            pltpu.SemaphoreType.DMA((4,)),
        ],
        compiler_params=pltpu.CompilerParams(vmem_limit_bytes=48 << 20),
        name="attend",
    )(lists, queries, out_grad, kloc, vloc, krem, vrem)


def requested_blocks(block_lists):
    me = lax.axis_index("ctx")
    flat = block_lists.reshape(-1)
    hits = jnp.any(flat[:, None] == jnp.arange(CTX * QB)[None, :], axis=0).reshape(CTX, QB)
    rank = jnp.cumsum(hits.astype(jnp.int32), axis=1) - 1
    pick = hits[:, :, None] & (rank[:, :, None] == jnp.arange(CAP)[None, None, :])
    return jnp.sum(jnp.where(pick, jnp.arange(QB)[None, :, None], 0), axis=1)


def per_device(queries, key_states, value_states, block_lists, out_grad):
    kloc, vloc = (
        lax.all_to_all(x, "head", split_axis=1, concat_axis=0, tiled=True)
        for x in (key_states, value_states)
    )
    asked = lax.all_to_all(requested_blocks(block_lists), "ctx", 0, 0, tiled=True).reshape(-1)
    krem, vrem = (
        lax.all_to_all(
            x.reshape(QB, BLK, HEAD_DIM)[asked].reshape(CTX, SLOT, HEAD_DIM), "ctx", 0, 0, tiled=True
        ).reshape(REM, HEAD_DIM)
        for x in (kloc, vloc)
    )
    att, dq, gkl, gvl, gkr, gvr = attend(
        block_lists, queries, out_grad, kloc, vloc, krem, vrem
    )
    me = lax.axis_index("ctx")
    later = jnp.repeat(jnp.arange(CTX) > me, CAP)[:, None, None]
    outs = []
    for local, remote in ((gkl, gkr), (gvl, gvr)):
        back = lax.all_to_all(remote.reshape(CTX, SLOT, HEAD_DIM), "ctx", 0, 0, tiled=True)
        back = back.reshape(CTX * CAP, BLK, HEAD_DIM).astype(jnp.float32)
        back = jnp.where(later, back, 0.0)
        total = local.reshape(QB, BLK, HEAD_DIM).at[asked].add(back).astype(jnp.bfloat16)
        outs.append(
            lax.all_to_all(total.reshape(TOK, HEAD_DIM), "head", 0, 1, tiled=True)
        )
    return att, dq, outs[0], outs[1]


def solution(mesh):
    return jax.shard_map(
        per_device,
        mesh=mesh,
        in_specs=(
            P("ctx", "head"),
            P(("ctx", "head"), None),
            P(("ctx", "head"), None),
            P("ctx", None),
            P("ctx", "head"),
        ),
        out_specs=(
            P("ctx", "head"),
            P("ctx", "head"),
            P(("ctx", "head"), None),
            P(("ctx", "head"), None),
        ),
        check_vma=False,
    )
```

```python
import functools

import jax
import jax.numpy as jnp
from jax import lax
from jax.experimental import pallas as pl
from jax.experimental.pallas import tpu as pltpu
from jax.sharding import PartitionSpec as P

HEAD_DIM = 128
GROUP = 4
BLK = 64
LIST = 8
CAP = 3
QB = 16
ROWS = 4
COLS = 8
CTX = ROWS * COLS
HEADS_AX = 8
TOK = QB * BLK
SLOT = CAP * BLK
OWN = QB // HEADS_AX
REM = CTX * SLOT
ALL = TOK + REM
NEG_FILL = -1e30
SCALE = HEAD_DIM ** (-0.5)
LOG2E = 1.4426950408889634
STEP_BLOCKS = 2

NT = (((1,), (1,)), ((), ()))
TN = (((0,), (0,)), ((), ()))
NN = (((1,), (0,)), ((), ()))


def dot(a, b, dims):
    return lax.dot_general(a, b, dims, preferred_element_type=jnp.float32)


def attend_kernel(
    lists, q_ref, do_ref, kloc, vloc, krem, vrem,
    att_ref, dq_ref, gkl, gvl, gkr, gvr,
    kall, vall, gk, gv, masks, sems,
):
    step = pl.program_id(0)
    me = lax.axis_index("ctx")

    @pl.when(step == 0)
    def _():
        copies = [
            pltpu.make_async_copy(kloc, kall.at[pl.ds(0, TOK)], sems.at[0]),
            pltpu.make_async_copy(krem, kall.at[pl.ds(TOK, REM)], sems.at[1]),
            pltpu.make_async_copy(vloc, vall.at[pl.ds(0, TOK)], sems.at[2]),
            pltpu.make_async_copy(vrem, vall.at[pl.ds(TOK, REM)], sems.at[3]),
        ]
        for copy in copies:
            copy.start()

        def clear(i, _):
            rows = pl.ds(pl.multiple_of(i * 256, 256), 256)
            gk[rows] = jnp.zeros((256, HEAD_DIM), jnp.float32)
            gv[rows] = jnp.zeros((256, HEAD_DIM), jnp.float32)
            return 0

        lax.fori_loop(0, ALL // 256, clear, 0)
        for owner in range(CTX):
            masks[owner] = 0
        for i in range(QB):
            for j in range(1, LIST):
                ref = lists[i, j]
                owner = lax.shift_right_logical(ref, 4)
                masks[owner] = masks[owner] | lax.shift_left(jnp.int32(1), ref & 15)
        for copy in copies:
            copy.wait()

    key_row = lax.broadcasted_iota(jnp.int32, (BLK, GROUP * BLK), 0)
    query_col = lax.broadcasted_iota(jnp.int32, (BLK, GROUP * BLK), 1) % BLK
    hidden = jnp.where(key_row > query_col, NEG_FILL, 0.0).astype(jnp.float32)

    for u in range(STEP_BLOCKS):
        i = step * STEP_BLOCKS + u
        rows = pl.ds(u * BLK, BLK)
        starts, flags = [], []
        for j in range(LIST):
            ref = lists[i, j]
            owner = lax.shift_right_logical(ref, 4)
            inner = ref & 15
            below = masks[owner] & (lax.shift_left(jnp.int32(1), inner) - 1)
            rank = (below != 0).astype(jnp.int32) + ((below & (below - 1)) != 0).astype(jnp.int32)
            slot = jnp.where(owner == me, inner, QB + owner * CAP + rank)
            starts.append(pl.multiple_of(slot * BLK, BLK))
            flags.append((ref == me * QB + i).astype(jnp.float32))
        q = jnp.concatenate(
            [q_ref[rows, pl.ds(g * HEAD_DIM, HEAD_DIM)] for g in range(GROUP)], axis=0
        )
        do = jnp.concatenate(
            [do_ref[rows, pl.ds(g * HEAD_DIM, HEAD_DIM)] for g in range(GROUP)], axis=0
        )
        keys = jnp.concatenate([kall[pl.ds(s, BLK)] for s in starts], axis=0)
        values = jnp.concatenate([vall[pl.ds(s, BLK)] for s in starts], axis=0)
        raw = dot(keys, q, NT) * (SCALE * LOG2E)
        parts = []
        for j in range(LIST):
            part = raw[j * BLK : (j + 1) * BLK]
            parts.append(part + (hidden if j == 0 else hidden * flags[j]))
        scores = jnp.concatenate(parts, axis=0)
        peak = jnp.max(scores, axis=0, keepdims=True)
        expo = jnp.exp2(scores - peak)
        probs = expo * (1.0 / jnp.sum(expo, axis=0, keepdims=True))
        probs_low = probs.astype(jnp.bfloat16)
        dprob = dot(values, do, NT)
        weighted = probs * dprob
        delta = jnp.sum(weighted, axis=0, keepdims=True)
        dscore = (weighted - probs * delta).astype(jnp.bfloat16)
        att = jnp.transpose(dot(values, probs_low, TN)).astype(jnp.bfloat16)
        dq = (jnp.transpose(dot(keys, dscore, TN)) * SCALE).astype(jnp.bfloat16)
        for g in range(GROUP):
            att_ref[rows, pl.ds(g * HEAD_DIM, HEAD_DIM)] = att[g * BLK : (g + 1) * BLK]
            dq_ref[rows, pl.ds(g * HEAD_DIM, HEAD_DIM)] = dq[g * BLK : (g + 1) * BLK]
        dv = dot(probs_low, do, NN)
        dk = dot(dscore, q, NN)
        for j in range(LIST):
            here = pl.ds(starts[j], BLK)
            gk[here] += dk[j * BLK : (j + 1) * BLK]
            gv[here] += dv[j * BLK : (j + 1) * BLK]

    @pl.when(step == QB // STEP_BLOCKS - 1)
    def _():
        gkl[...] = gk[pl.ds(0, TOK)] * SCALE
        gvl[...] = gv[pl.ds(0, TOK)]

        def put(o, _):
            src = pl.ds(pl.multiple_of(TOK + o * SLOT, BLK), SLOT)
            dst = pl.ds(pl.multiple_of(o * SLOT, BLK), SLOT)
            gkr[dst] = (gk[src] * SCALE).astype(jnp.bfloat16)
            gvr[dst] = gv[src].astype(jnp.bfloat16)
            return 0

        lax.fori_loop(0, me, put, 0)


def attend(lists, queries, out_grad, kloc, vloc, krem, vrem):
    bf16, f32 = jnp.bfloat16, jnp.float32
    wide = GROUP * HEAD_DIM
    tile = pl.BlockSpec((STEP_BLOCKS * BLK, wide), lambda s: (s, 0))
    whole = lambda n: pl.BlockSpec((n, HEAD_DIM), lambda s: (0, 0), pipeline_mode=pl.Buffered(1))
    anywhere = pl.BlockSpec(memory_space=pl.ANY)
    return pl.pallas_call(
        attend_kernel,
        grid=(QB // STEP_BLOCKS,),
        in_specs=[pl.BlockSpec(memory_space=pltpu.SMEM), tile, tile] + [anywhere] * 4,
        out_specs=[tile, tile, whole(TOK), whole(TOK), whole(REM), whole(REM)],
        out_shape=[
            jax.ShapeDtypeStruct((TOK, wide), bf16),
            jax.ShapeDtypeStruct((TOK, wide), bf16),
            jax.ShapeDtypeStruct((TOK, HEAD_DIM), f32),
            jax.ShapeDtypeStruct((TOK, HEAD_DIM), f32),
            jax.ShapeDtypeStruct((REM, HEAD_DIM), bf16),
            jax.ShapeDtypeStruct((REM, HEAD_DIM), bf16),
        ],
        scratch_shapes=[
            pltpu.VMEM((ALL, HEAD_DIM), bf16),
            pltpu.VMEM((ALL, HEAD_DIM), bf16),
            pltpu.VMEM((ALL, HEAD_DIM), f32),
            pltpu.VMEM((ALL, HEAD_DIM), f32),
            pltpu.SMEM((CTX,), jnp.int32),
            pltpu.SemaphoreType.DMA((4,)),
        ],
        compiler_params=pltpu.CompilerParams(vmem_limit_bytes=48 << 20),
        name="attend",
    )(lists, queries, out_grad, kloc, vloc, krem, vrem)


def here():
    me = lax.axis_index("ctx")
    return lax.axis_index("head"), me, me // COLS, me % COLS


def slot_rows(index):
    return pl.ds(pl.multiple_of(index * SLOT, BLK), SLOT)


def remote(src, dst, send_sem, recv_sem, **device):
    return pltpu.make_async_remote_copy(
        src_ref=src,
        dst_ref=dst,
        send_sem=send_sem,
        recv_sem=recv_sem,
        device_id=device,
        device_id_type=pl.DeviceIdType.MESH,
    )


def greet(with_heads, with_ctx):
    head, me, y, z = here()
    barrier = pltpu.get_barrier_semaphore()
    peers = []
    if with_heads:
        peers += [{"head": (head + k) % HEADS_AX} for k in range(1, HEADS_AX)]
    if with_ctx:
        peers += [{"ctx": y * COLS + (z + k) % COLS} for k in range(1, COLS)]
        peers += [{"ctx": (y + k) % ROWS * COLS + z} for k in range(1, ROWS)]
    for peer in peers:
        pl.semaphore_signal(barrier, inc=1, device_id=peer, device_id_type=pl.DeviceIdType.MESH)
    pl.semaphore_wait(barrier, len(peers))


def along_first(dr, kv):
    return dr >= 2 + kv


def exchange(sign, prepare, source, slots, relays, first_send, relay_recv, relay_send, slot_recv):
    _, me, y, z = here()

    def inside(value, limit):
        return jnp.logical_and(value >= 0, value < limit)

    def send_copy(kv, dr, k):
        row, col = y + sign * dr, (z + sign * k + COLS) % COLS
        src = source(kv, dr, k, row * COLS + col)
        send = first_send.at[kv, dr, k]
        if dr == 0:
            return remote(src, slots[kv].at[slot_rows(me)], send, slot_recv.at[kv, me], ctx=y * COLS + col)
        if isinstance(k, int) and k == 0:
            return remote(src, slots[kv].at[slot_rows(me)], send, slot_recv.at[kv, me], ctx=row * COLS + z)
        target = y * COLS + col if along_first(dr, kv) else row * COLS + z
        return remote(
            src, relays[kv].at[dr - 1, k], send, relay_recv.at[kv, dr - 1, k], ctx=target
        )

    def sent(dr, k):
        if dr == 0:
            return inside(z + sign * k, COLS)
        return inside(y + sign * dr, ROWS)

    def start(dr, k):
        @pl.when(sent(dr, k))
        def _():
            prepare(dr, k, (y + sign * dr) * COLS + (z + sign * k + COLS) % COLS)
            for kv in range(2):
                send_copy(kv, dr, k).start()

    def relay_copy(kv, dr, k):
        if along_first(dr, kv):
            origin = y * COLS + (z - sign * k + COLS) % COLS
            target = (y + sign * dr) * COLS + z
        else:
            origin = (y - sign * dr) * COLS + z
            target = y * COLS + (z + sign * k + COLS) % COLS
        return remote(
            relays[kv].at[dr - 1, k],
            slots[kv].at[slot_rows(origin)],
            relay_send.at[kv, dr - 1, k],
            slot_recv.at[kv, origin],
            ctx=target,
        )

    def relayed(kv, dr):
        return inside(y + sign * dr if along_first(dr, kv) else y - sign * dr, ROWS)

    def arrival(kv, dr, k):
        return remote(
            relays[kv].at[dr - 1, k],
            relays[kv].at[dr - 1, k],
            relay_send.at[kv, dr - 1, k],
            relay_recv.at[kv, dr - 1, k],
            ctx=me,
        )

    def slot_wait(kv, origin):
        rows = slot_rows(origin)
        remote(
            slots[kv].at[rows], slots[kv].at[rows], first_send.at[kv, 0, 0], slot_recv.at[kv, origin], ctx=me
        ).wait_recv()

    def send_step(k, _):
        for dr in (3, 2, 1, 0):
            start(dr, k)
        return 0

    def relay_step(k, _):
        for dr in (3, 2, 1):
            for kv in range(2):

                @pl.when(relayed(kv, dr))
                def _(kv=kv, dr=dr):
                    arrival(kv, dr, k).wait_recv()
                    relay_copy(kv, dr, k).start()

        return 0

    def finish_step(k, _):
        @pl.when(inside(z - sign * k, COLS))
        def _():
            for kv in range(2):
                slot_wait(kv, y * COLS + z - sign * k)

        for dr in (1, 2, 3):

            @pl.when(inside(y - sign * dr, ROWS))
            def _(dr=dr):
                for kv in range(2):
                    slot_wait(kv, (y - sign * dr) * COLS + (z - sign * k + COLS) % COLS)

            for kv in range(2):

                @pl.when(relayed(kv, dr))
                def _(kv=kv, dr=dr):
                    relay_copy(kv, dr, k).wait_send()

        for dr in range(ROWS):

            @pl.when(sent(dr, k))
            def _(dr=dr):
                for kv in range(2):
                    send_copy(kv, dr, k).wait_send()

        return 0

    lax.fori_loop(1, COLS, send_step, 0)
    for dr in (3, 2, 1):
        start(dr, 0)
    lax.fori_loop(1, COLS, relay_step, 0)
    lax.fori_loop(1, COLS, finish_step, 0)
    for dr in (1, 2, 3):

        @pl.when(inside(y - sign * dr, ROWS))
        def _(dr=dr):
            for kv in range(2):
                slot_wait(kv, (y - sign * dr) * COLS + z)

        @pl.when(sent(dr, 0))
        def _(dr=dr):
            for kv in range(2):
                send_copy(kv, dr, 0).wait_send()


EXCHANGE_SCRATCH = [
    pltpu.VMEM((ROWS - 1, COLS, SLOT, HEAD_DIM), jnp.bfloat16),
    pltpu.VMEM((ROWS - 1, COLS, SLOT, HEAD_DIM), jnp.bfloat16),
    pltpu.SemaphoreType.DMA((2, ROWS, COLS)),
    pltpu.SemaphoreType.DMA((2, ROWS - 1, COLS)),
    pltpu.SemaphoreType.DMA((2, ROWS - 1, COLS)),
    pltpu.SemaphoreType.DMA((2, CTX)),
]


def lowest_bit_index(bits):
    low = bits & (-bits)
    index = jnp.where((low & 0xAAAA) != 0, 1, 0)
    index += jnp.where((low & 0xCCCC) != 0, 2, 0)
    index += jnp.where((low & 0xF0F0) != 0, 4, 0)
    index += jnp.where((low & 0xFF00) != 0, 8, 0)
    return index, bits & (bits - 1)


def fetch_kernel(
    lists, key_in, value_in, kloc, vloc, krem, vrem, table,
    asked, kstage, vstage, krelay, vrelay, first_send, relay_recv, relay_send, slot_recv,
    head_send, head_recv, table_send, table_recv, local_sem,
):
    head, me, y, z = here()
    greet(True, True)
    sides = ((key_in, kloc), (value_in, vloc))

    def head_copy(kv, k):
        src, dst = sides[kv]
        peer = (head + k) % HEADS_AX
        cols = pl.ds(pl.multiple_of(peer * HEAD_DIM, HEAD_DIM), HEAD_DIM)
        mine = pl.ds(head * OWN, OWN)
        if k == 0:
            return pltpu.make_async_copy(src.at[:, :, cols], dst.at[mine], local_sem.at[kv])
        return remote(
            src.at[:, :, cols], dst.at[mine], head_send.at[kv, k], head_recv.at[kv, head], head=peer
        )

    def head_arrival(kv, k):
        peer = (head + HEADS_AX - k) % HEADS_AX
        dst = sides[kv][1].at[pl.ds(peer * OWN, OWN)]
        return remote(dst, dst, head_send.at[kv, k], head_recv.at[kv, peer], head=head)

    for k in (4, 3, 5, 2, 6, 1, 7, 0):
        for kv in range(2):
            head_copy(kv, k).start()

    lane = lax.broadcasted_iota(jnp.int32, (1, 128), 1)
    wanted = jnp.zeros((1, 128), jnp.int32)
    for i in range(QB):
        for j in range(1, LIST):
            ref = lists[i, j]
            low, high = ref & 3, lax.shift_right_logical(ref, 2) & 3
            bit = (1 + (low & 1)) * (1 + 3 * lax.shift_right_logical(low, 1))
            bit = bit * (1 + 15 * (high & 1)) * (1 + 255 * lax.shift_right_logical(high, 1))
            wanted = wanted | jnp.where(lane == lax.shift_right_logical(ref, 4), bit, 0)
    first, rest = lowest_bit_index(wanted)
    second, rest = lowest_bit_index(rest)
    third, rest = lowest_bit_index(rest)
    table[me] = first + second * 16 + third * 256

    def along_row(k):
        return remote(
            table.at[me], table.at[me], table_send.at[k], table_recv.at[z], ctx=y * COLS + (z + k) % COLS
        )

    def along_row_wait(k):
        origin = (z + COLS - k) % COLS
        ref = table.at[y * COLS + origin]
        remote(ref, ref, table_send.at[k], table_recv.at[origin], ctx=me).wait_recv()

    def rows_of(row):
        return table.at[pl.ds(row * COLS, COLS)]

    def across_rows(k):
        return remote(
            rows_of(y), rows_of(y), table_send.at[COLS + k], table_recv.at[COLS + y],
            ctx=(y + k) % ROWS * COLS + z,
        )

    for k in range(1, COLS):
        along_row(k).start()
    for k in range(1, COLS):
        along_row_wait(k)
    for k in range(1, ROWS):
        across_rows(k).start()
    for k in range(1, ROWS):
        row = (y + ROWS - k) % ROWS
        remote(
            rows_of(row), rows_of(row), table_send.at[COLS + k], table_recv.at[COLS + row], ctx=me
        ).wait_recv()
    for k in range(1, COLS):
        along_row(k).wait_send()
    for k in range(1, ROWS):
        across_rows(k).wait_send()
    to_scalar = pltpu.make_async_copy(table, asked, local_sem.at[2])
    to_scalar.start()
    for k in range(1, HEADS_AX):
        for kv in range(2):
            head_arrival(kv, k).wait_recv()
    for kv in range(2):
        head_copy(kv, 0).wait()
    to_scalar.wait()

    stages = (kstage, vstage)

    def prepare(dr, k, dest):
        packed = asked[dest, 0, me]
        for j in range(CAP):
            block = lax.shift_right_logical(packed, 4 * j) & 15
            for kv in range(2):
                stages[kv][dr, k, pl.ds(j * BLK, BLK), :] = sides[kv][1][block]

    def source(kv, dr, k, dest):
        return stages[kv].at[dr, k]

    exchange(
        1, prepare, source, (krem, vrem), (krelay, vrelay),
        first_send, relay_recv, relay_send, slot_recv,
    )
    for k in range(1, HEADS_AX):
        for kv in range(2):
            head_copy(kv, k).wait_send()


def fetch(lists, key_states, value_states):
    bf16 = jnp.bfloat16
    vmem = pl.BlockSpec(memory_space=pltpu.VMEM)
    anywhere = pl.BlockSpec(memory_space=pl.ANY)
    stage = pltpu.VMEM((ROWS, COLS, SLOT, HEAD_DIM), bf16)
    return pl.pallas_call(
        fetch_kernel,
        in_specs=[pl.BlockSpec(memory_space=pltpu.SMEM), anywhere, anywhere],
        out_specs=[vmem] * 5,
        out_shape=[
            jax.ShapeDtypeStruct((QB, BLK, HEAD_DIM), bf16),
            jax.ShapeDtypeStruct((QB, BLK, HEAD_DIM), bf16),
            jax.ShapeDtypeStruct((REM, HEAD_DIM), bf16),
            jax.ShapeDtypeStruct((REM, HEAD_DIM), bf16),
            jax.ShapeDtypeStruct((CTX, 1, 128), jnp.int32),
        ],
        scratch_shapes=[pltpu.SMEM((CTX, 1, 128), jnp.int32), stage, stage]
        + EXCHANGE_SCRATCH
        + [
            pltpu.SemaphoreType.DMA((2, HEADS_AX)),
            pltpu.SemaphoreType.DMA((2, HEADS_AX)),
            pltpu.SemaphoreType.DMA((COLS + ROWS,)),
            pltpu.SemaphoreType.DMA((COLS + ROWS,)),
            pltpu.SemaphoreType.DMA((3,)),
        ],
        compiler_params=pltpu.CompilerParams(
            collective_id=0, has_side_effects=True, vmem_limit_bytes=40 << 20
        ),
        name="fetch",
    )(lists, key_states, value_states)


def give_back_kernel(
    gkr, gvr, bk, bv, krelay, vrelay, first_send, relay_recv, relay_send, slot_recv
):
    greet(False, True)
    grads = (gkr, gvr)

    def source(kv, dr, k, dest):
        return grads[kv].at[slot_rows(dest)]

    exchange(
        -1, lambda dr, k, dest: None, source, (bk, bv), (krelay, vrelay),
        first_send, relay_recv, relay_send, slot_recv,
    )


def give_back(gkr, gvr):
    vmem = pl.BlockSpec(memory_space=pltpu.VMEM)
    return pl.pallas_call(
        give_back_kernel,
        in_specs=[vmem] * 2,
        out_specs=[vmem] * 2,
        out_shape=[jax.ShapeDtypeStruct((REM, HEAD_DIM), jnp.bfloat16)] * 2,
        scratch_shapes=EXCHANGE_SCRATCH,
        compiler_params=pltpu.CompilerParams(
            collective_id=1, has_side_effects=True, vmem_limit_bytes=40 << 20
        ),
        name="give_back",
    )(gkr, gvr)


def add_up_kernel(asked, gkl, gvl, bk, bv, kout, vout, kacc, vacc):
    me = lax.axis_index("ctx")
    kacc[...] = gkl[...]
    vacc[...] = gvl[...]

    def step(origin, _):
        packed = asked[origin, 0, me]
        for j in range(CAP):
            block = lax.shift_right_logical(packed, 4 * j) & 15
            rows = pl.ds(pl.multiple_of(block * BLK, BLK), BLK)
            came = pl.ds(pl.multiple_of(origin * SLOT + j * BLK, BLK), BLK)
            kacc[rows] += bk[came].astype(jnp.float32)
            vacc[rows] += bv[came].astype(jnp.float32)
        return 0

    lax.fori_loop(me + 1, CTX, step, 0)
    kout[...] = kacc[...].astype(jnp.bfloat16)
    vout[...] = vacc[...].astype(jnp.bfloat16)


def add_up(table, gkl, gvl, bk, bv):
    vmem = pl.BlockSpec(memory_space=pltpu.VMEM)
    return pl.pallas_call(
        add_up_kernel,
        in_specs=[pl.BlockSpec(memory_space=pltpu.SMEM)] + [vmem] * 4,
        out_specs=[vmem] * 2,
        out_shape=[jax.ShapeDtypeStruct((TOK, HEAD_DIM), jnp.bfloat16)] * 2,
        scratch_shapes=[pltpu.VMEM((TOK, HEAD_DIM), jnp.float32)] * 2,
        compiler_params=pltpu.CompilerParams(vmem_limit_bytes=40 << 20),
        name="add_up",
    )(table, gkl, gvl, bk, bv)


def spread_kernel(kg, vg, kout, vout, head_send, head_recv, local_sem):
    head = lax.axis_index("head")
    greet(True, False)
    sides = ((kg, kout), (vg, vout))
    mine = pl.ds(pl.multiple_of(head * HEAD_DIM, HEAD_DIM), HEAD_DIM)

    def copy(kv, k):
        src, dst = sides[kv]
        peer = (head + k) % HEADS_AX
        rows = src.at[pl.ds(pl.multiple_of(peer * HEAD_DIM, HEAD_DIM), HEAD_DIM)]
        if k == 0:
            return pltpu.make_async_copy(rows, dst.at[:, mine], local_sem.at[kv])
        return remote(rows, dst.at[:, mine], head_send.at[kv, k], head_recv.at[kv, head], head=peer)

    def arrival(kv, k):
        peer = (head + HEADS_AX - k) % HEADS_AX
        cols = pl.ds(pl.multiple_of(peer * HEAD_DIM, HEAD_DIM), HEAD_DIM)
        ref = sides[kv][1].at[:, cols]
        return remote(ref, ref, head_send.at[kv, k], head_recv.at[kv, peer], head=head)

    order = (4, 3, 5, 2, 6, 1, 7)
    for k in order:
        for kv in range(2):
            copy(kv, k).start()
    for kv in range(2):
        copy(kv, 0).start()
    for k in order:
        for kv in range(2):
            copy(kv, k).wait_send()
            arrival(kv, k).wait_recv()
    for kv in range(2):
        copy(kv, 0).wait()


def spread(kg, vg):
    vmem = pl.BlockSpec(memory_space=pltpu.VMEM)
    return pl.pallas_call(
        spread_kernel,
        in_specs=[vmem] * 2,
        out_specs=[vmem] * 2,
        out_shape=[jax.ShapeDtypeStruct((TOK // HEADS_AX, HEADS_AX * HEAD_DIM), jnp.bfloat16)] * 2,
        scratch_shapes=[
            pltpu.SemaphoreType.DMA((2, HEADS_AX)),
            pltpu.SemaphoreType.DMA((2, HEADS_AX)),
            pltpu.SemaphoreType.DMA((2,)),
        ],
        compiler_params=pltpu.CompilerParams(collective_id=2, has_side_effects=True),
        name="spread",
    )(kg, vg)


def per_device(queries, key_states, value_states, block_lists, out_grad):
    by_block = (OWN, BLK, HEADS_AX * HEAD_DIM)
    kloc, vloc, krem, vrem, table = fetch(
        block_lists, key_states.reshape(by_block), value_states.reshape(by_block)
    )
    kloc, vloc = kloc.reshape(TOK, HEAD_DIM), vloc.reshape(TOK, HEAD_DIM)
    att, dq, gkl, gvl, gkr, gvr = attend(
        block_lists, queries, out_grad, kloc, vloc, krem, vrem
    )
    bk, bv = give_back(gkr, gvr)
    kg, vg = add_up(table, gkl, gvl, bk, bv)
    key_grad, value_grad = spread(kg, vg)
    return att, dq, key_grad, value_grad


def solution(mesh):
    return jax.shard_map(
        per_device,
        mesh=mesh,
        in_specs=(
            P("ctx", "head"),
            P(("ctx", "head"), None),
            P(("ctx", "head"), None),
            P("ctx", None),
            P("ctx", "head"),
        ),
        out_specs=(
            P("ctx", "head"),
            P("ctx", "head"),
            P(("ctx", "head"), None),
            P(("ctx", "head"), None),
        ),
        check_vma=False,
    )
```

```python
import functools

import jax
import jax.numpy as jnp
from jax import lax
from jax.experimental import pallas as pl
from jax.experimental.pallas import tpu as pltpu
from jax.sharding import PartitionSpec as P

HEAD_DIM = 128
GROUP = 4
BLK = 64
LIST = 8
CAP = 3
QB = 16
ROWS = 4
COLS = 8
CTX = ROWS * COLS
HEADS_AX = 8
TOK = QB * BLK
SLOT = CAP * BLK
OWN = QB // HEADS_AX
REM = CTX * SLOT
ALL = TOK + REM
NEG_FILL = -1e30
SCALE = HEAD_DIM ** (-0.5)
LOG2E = 1.4426950408889634
STEP_BLOCKS = 2

NT = (((1,), (1,)), ((), ()))
TN = (((0,), (0,)), ((), ()))
NN = (((1,), (0,)), ((), ()))


def dot(a, b, dims):
    return lax.dot_general(a, b, dims, preferred_element_type=jnp.float32)


def attend_kernel(
    lists, q_ref, do_ref, kloc, vloc, krem, vrem,
    att_ref, dq_ref, gkl, gvl, gkr, gvr,
    kall, vall, gk, gv, masks, sems,
):
    step = pl.program_id(0)
    me = lax.axis_index("ctx")

    @pl.when(step == 0)
    def _():
        copies = [
            pltpu.make_async_copy(kloc, kall.at[pl.ds(0, TOK)], sems.at[0]),
            pltpu.make_async_copy(krem, kall.at[pl.ds(TOK, REM)], sems.at[1]),
            pltpu.make_async_copy(vloc, vall.at[pl.ds(0, TOK)], sems.at[2]),
            pltpu.make_async_copy(vrem, vall.at[pl.ds(TOK, REM)], sems.at[3]),
        ]
        for copy in copies:
            copy.start()

        def clear(i, _):
            rows = pl.ds(pl.multiple_of(i * 256, 256), 256)
            gk[rows] = jnp.zeros((256, HEAD_DIM), jnp.float32)
            gv[rows] = jnp.zeros((256, HEAD_DIM), jnp.float32)
            return 0

        lax.fori_loop(0, ALL // 256, clear, 0)
        for owner in range(CTX):
            masks[owner] = 0
        for i in range(QB):
            for j in range(1, LIST):
                ref = lists[i, j]
                owner = lax.shift_right_logical(ref, 4)
                masks[owner] = masks[owner] | lax.shift_left(jnp.int32(1), ref & 15)
        for copy in copies:
            copy.wait()

    key_row = lax.broadcasted_iota(jnp.int32, (BLK, GROUP * BLK), 0)
    query_col = lax.broadcasted_iota(jnp.int32, (BLK, GROUP * BLK), 1) % BLK
    hidden = jnp.where(key_row > query_col, NEG_FILL, 0.0).astype(jnp.float32)

    for u in range(STEP_BLOCKS):
        i = step * STEP_BLOCKS + u
        rows = pl.ds(u * BLK, BLK)
        starts, flags = [], []
        for j in range(LIST):
            ref = lists[i, j]
            owner = lax.shift_right_logical(ref, 4)
            inner = ref & 15
            below = masks[owner] & (lax.shift_left(jnp.int32(1), inner) - 1)
            rank = (below != 0).astype(jnp.int32) + ((below & (below - 1)) != 0).astype(jnp.int32)
            slot = jnp.where(owner == me, inner, QB + owner * CAP + rank)
            starts.append(pl.multiple_of(slot * BLK, BLK))
            flags.append((ref == me * QB + i).astype(jnp.float32))
        q = jnp.concatenate(
            [q_ref[rows, pl.ds(g * HEAD_DIM, HEAD_DIM)] for g in range(GROUP)], axis=0
        )
        do = jnp.concatenate(
            [do_ref[rows, pl.ds(g * HEAD_DIM, HEAD_DIM)] for g in range(GROUP)], axis=0
        )
        keys = jnp.concatenate([kall[pl.ds(s, BLK)] for s in starts], axis=0)
        values = jnp.concatenate([vall[pl.ds(s, BLK)] for s in starts], axis=0)
        raw = dot(keys, q, NT) * (SCALE * LOG2E)
        parts = []
        for j in range(LIST):
            part = raw[j * BLK : (j + 1) * BLK]
            parts.append(part + (hidden if j == 0 else hidden * flags[j]))
        scores = jnp.concatenate(parts, axis=0)
        peak = jnp.max(scores, axis=0, keepdims=True)
        expo = jnp.exp2(scores - peak)
        probs = expo * (1.0 / jnp.sum(expo, axis=0, keepdims=True))
        probs_low = probs.astype(jnp.bfloat16)
        dprob = dot(values, do, NT)
        weighted = probs * dprob
        delta = jnp.sum(weighted, axis=0, keepdims=True)
        dscore = (weighted - probs * delta).astype(jnp.bfloat16)
        att = jnp.transpose(dot(values, probs_low, TN)).astype(jnp.bfloat16)
        dq = (jnp.transpose(dot(keys, dscore, TN)) * SCALE).astype(jnp.bfloat16)
        for g in range(GROUP):
            att_ref[rows, pl.ds(g * HEAD_DIM, HEAD_DIM)] = att[g * BLK : (g + 1) * BLK]
            dq_ref[rows, pl.ds(g * HEAD_DIM, HEAD_DIM)] = dq[g * BLK : (g + 1) * BLK]
        dv = dot(probs_low, do, NN)
        dk = dot(dscore, q, NN)
        for j in range(LIST):
            here = pl.ds(starts[j], BLK)
            gk[here] += dk[j * BLK : (j + 1) * BLK]
            gv[here] += dv[j * BLK : (j + 1) * BLK]

    @pl.when(step == QB // STEP_BLOCKS - 1)
    def _():
        gkl[...] = gk[pl.ds(0, TOK)] * SCALE
        gvl[...] = gv[pl.ds(0, TOK)]

        def put(o, _):
            src = pl.ds(pl.multiple_of(TOK + o * SLOT, BLK), SLOT)
            dst = pl.ds(pl.multiple_of(o * SLOT, BLK), SLOT)
            gkr[dst] = (gk[src] * SCALE).astype(jnp.bfloat16)
            gvr[dst] = gv[src].astype(jnp.bfloat16)
            return 0

        lax.fori_loop(0, me, put, 0)


def attend(lists, queries, out_grad, kloc, vloc, krem, vrem):
    bf16, f32 = jnp.bfloat16, jnp.float32
    wide = GROUP * HEAD_DIM
    tile = pl.BlockSpec((STEP_BLOCKS * BLK, wide), lambda s: (s, 0))
    whole = lambda n: pl.BlockSpec((n, HEAD_DIM), lambda s: (0, 0), pipeline_mode=pl.Buffered(1))
    anywhere = pl.BlockSpec(memory_space=pl.ANY)
    return pl.pallas_call(
        attend_kernel,
        grid=(QB // STEP_BLOCKS,),
        in_specs=[pl.BlockSpec(memory_space=pltpu.SMEM), tile, tile] + [anywhere] * 4,
        out_specs=[tile, tile, whole(TOK), whole(TOK), whole(REM), whole(REM)],
        out_shape=[
            jax.ShapeDtypeStruct((TOK, wide), bf16),
            jax.ShapeDtypeStruct((TOK, wide), bf16),
            jax.ShapeDtypeStruct((TOK, HEAD_DIM), f32),
            jax.ShapeDtypeStruct((TOK, HEAD_DIM), f32),
            jax.ShapeDtypeStruct((REM, HEAD_DIM), bf16),
            jax.ShapeDtypeStruct((REM, HEAD_DIM), bf16),
        ],
        scratch_shapes=[
            pltpu.VMEM((ALL, HEAD_DIM), bf16),
            pltpu.VMEM((ALL, HEAD_DIM), bf16),
            pltpu.VMEM((ALL, HEAD_DIM), f32),
            pltpu.VMEM((ALL, HEAD_DIM), f32),
            pltpu.SMEM((CTX,), jnp.int32),
            pltpu.SemaphoreType.DMA((4,)),
        ],
        compiler_params=pltpu.CompilerParams(vmem_limit_bytes=30 << 20),
        name="attend",
    )(lists, queries, out_grad, kloc, vloc, krem, vrem)


def here():
    me = lax.axis_index("ctx")
    return lax.axis_index("head"), me, me // COLS, me % COLS


def slot_rows(index):
    return pl.ds(pl.multiple_of(index * SLOT, BLK), SLOT)


def remote(src, dst, send_sem, recv_sem, **device):
    return pltpu.make_async_remote_copy(
        src_ref=src,
        dst_ref=dst,
        send_sem=send_sem,
        recv_sem=recv_sem,
        device_id=device,
        device_id_type=pl.DeviceIdType.MESH,
    )


def greet(with_heads, with_ctx):
    head, me, y, z = here()
    barrier = pltpu.get_barrier_semaphore()
    peers = []
    if with_heads:
        peers += [{"head": (head + k) % HEADS_AX} for k in range(1, HEADS_AX)]
    if with_ctx:
        peers += [{"ctx": y * COLS + (z + k) % COLS} for k in range(1, COLS)]
        peers += [{"ctx": (y + k) % ROWS * COLS + z} for k in range(1, ROWS)]
    for peer in peers:
        pl.semaphore_signal(barrier, inc=1, device_id=peer, device_id_type=pl.DeviceIdType.MESH)
    pl.semaphore_wait(barrier, len(peers))


def along_first(dr, kv):
    return dr >= 2 + kv


def exchange(sign, prepare, source, slots, relays, first_send, relay_recv, relay_send, slot_recv):
    _, me, y, z = here()

    def inside(value, limit):
        return jnp.logical_and(value >= 0, value < limit)

    def send_copy(kv, dr, k):
        row, col = y + sign * dr, (z + sign * k + COLS) % COLS
        src = source(kv, dr, k, row * COLS + col)
        send = first_send.at[kv, dr, k]
        if dr == 0:
            return remote(src, slots[kv].at[slot_rows(me)], send, slot_recv.at[kv, me], ctx=y * COLS + col)
        if isinstance(k, int) and k == 0:
            return remote(src, slots[kv].at[slot_rows(me)], send, slot_recv.at[kv, me], ctx=row * COLS + z)
        target = y * COLS + col if along_first(dr, kv) else row * COLS + z
        return remote(
            src, relays[kv].at[dr - 1, k], send, relay_recv.at[kv, dr - 1, k], ctx=target
        )

    def sent(dr, k):
        if dr == 0:
            return inside(z + sign * k, COLS)
        return inside(y + sign * dr, ROWS)

    def start(dr, k):
        @pl.when(sent(dr, k))
        def _():
            prepare(dr, k, (y + sign * dr) * COLS + (z + sign * k + COLS) % COLS)
            for kv in range(2):
                send_copy(kv, dr, k).start()

    def relay_copy(kv, dr, k):
        if along_first(dr, kv):
            origin = y * COLS + (z - sign * k + COLS) % COLS
            target = (y + sign * dr) * COLS + z
        else:
            origin = (y - sign * dr) * COLS + z
            target = y * COLS + (z + sign * k + COLS) % COLS
        return remote(
            relays[kv].at[dr - 1, k],
            slots[kv].at[slot_rows(origin)],
            relay_send.at[kv, dr - 1, k],
            slot_recv.at[kv, origin],
            ctx=target,
        )

    def relayed(kv, dr):
        return inside(y + sign * dr if along_first(dr, kv) else y - sign * dr, ROWS)

    def arrival(kv, dr, k):
        return remote(
            relays[kv].at[dr - 1, k],
            relays[kv].at[dr - 1, k],
            relay_send.at[kv, dr - 1, k],
            relay_recv.at[kv, dr - 1, k],
            ctx=me,
        )

    def slot_wait(kv, origin):
        rows = slot_rows(origin)
        remote(
            slots[kv].at[rows], slots[kv].at[rows], first_send.at[kv, 0, 0], slot_recv.at[kv, origin], ctx=me
        ).wait_recv()

    def cross_step(k, _):
        for dr in (3, 2, 1):
            start(dr, k)
        return 0

    def own_step(k, _):
        start(0, k)
        return 0

    def relay_step(k, _):
        for dr in (3, 2, 1):
            for kv in range(2):

                @pl.when(relayed(kv, dr))
                def _(kv=kv, dr=dr):
                    arrival(kv, dr, k).wait_recv()
                    relay_copy(kv, dr, k).start()

        return 0

    def finish_step(k, _):
        @pl.when(inside(z - sign * k, COLS))
        def _():
            for kv in range(2):
                slot_wait(kv, y * COLS + z - sign * k)

        for dr in (1, 2, 3):

            @pl.when(inside(y - sign * dr, ROWS))
            def _(dr=dr):
                for kv in range(2):
                    slot_wait(kv, (y - sign * dr) * COLS + (z - sign * k + COLS) % COLS)

            for kv in range(2):

                @pl.when(relayed(kv, dr))
                def _(kv=kv, dr=dr):
                    relay_copy(kv, dr, k).wait_send()

        for dr in range(ROWS):

            @pl.when(sent(dr, k))
            def _(dr=dr):
                for kv in range(2):
                    send_copy(kv, dr, k).wait_send()

        return 0

    lax.fori_loop(1, COLS, cross_step, 0)
    for dr in (3, 2, 1):
        start(dr, 0)
    lax.fori_loop(1, COLS, own_step, 0)
    lax.fori_loop(1, COLS, relay_step, 0)
    lax.fori_loop(1, COLS, finish_step, 0)
    for dr in (1, 2, 3):

        @pl.when(inside(y - sign * dr, ROWS))
        def _(dr=dr):
            for kv in range(2):
                slot_wait(kv, (y - sign * dr) * COLS + z)

        @pl.when(sent(dr, 0))
        def _(dr=dr):
            for kv in range(2):
                send_copy(kv, dr, 0).wait_send()


EXCHANGE_SCRATCH = [
    pltpu.VMEM((ROWS - 1, COLS, SLOT, HEAD_DIM), jnp.bfloat16),
    pltpu.VMEM((ROWS - 1, COLS, SLOT, HEAD_DIM), jnp.bfloat16),
    pltpu.SemaphoreType.DMA((2, ROWS, COLS)),
    pltpu.SemaphoreType.DMA((2, ROWS - 1, COLS)),
    pltpu.SemaphoreType.DMA((2, ROWS - 1, COLS)),
    pltpu.SemaphoreType.DMA((2, CTX)),
]


def lowest_bit_index(bits):
    low = bits & (-bits)
    index = jnp.where((low & 0xAAAA) != 0, 1, 0)
    index += jnp.where((low & 0xCCCC) != 0, 2, 0)
    index += jnp.where((low & 0xF0F0) != 0, 4, 0)
    index += jnp.where((low & 0xFF00) != 0, 8, 0)
    return index, bits & (bits - 1)


def fetch_kernel(
    lists, key_in, value_in, kloc, vloc, krem, vrem, table,
    asked, kstage, vstage, krelay, vrelay, first_send, relay_recv, relay_send, slot_recv,
    head_send, head_recv, table_send, table_recv, local_sem,
):
    head, me, y, z = here()
    greet(True, True)
    sides = ((key_in, kloc), (value_in, vloc))

    def head_copy(kv, k):
        src, dst = sides[kv]
        peer = (head + k) % HEADS_AX
        cols = pl.ds(pl.multiple_of(peer * HEAD_DIM, HEAD_DIM), HEAD_DIM)
        mine = pl.ds(head * OWN, OWN)
        if k == 0:
            return pltpu.make_async_copy(src.at[:, :, cols], dst.at[mine], local_sem.at[kv])
        return remote(
            src.at[:, :, cols], dst.at[mine], head_send.at[kv, k], head_recv.at[kv, head], head=peer
        )

    def head_arrival(kv, k):
        peer = (head + HEADS_AX - k) % HEADS_AX
        dst = sides[kv][1].at[pl.ds(peer * OWN, OWN)]
        return remote(dst, dst, head_send.at[kv, k], head_recv.at[kv, peer], head=head)

    for k in (4, 3, 5, 2, 6, 1, 7, 0):
        for kv in range(2):
            head_copy(kv, k).start()

    lane = lax.broadcasted_iota(jnp.int32, (1, 128), 1)
    wanted = jnp.zeros((1, 128), jnp.int32)
    for i in range(QB):
        for j in range(1, LIST):
            ref = lists[i, j]
            low, high = ref & 3, lax.shift_right_logical(ref, 2) & 3
            bit = (1 + (low & 1)) * (1 + 3 * lax.shift_right_logical(low, 1))
            bit = bit * (1 + 15 * (high & 1)) * (1 + 255 * lax.shift_right_logical(high, 1))
            wanted = wanted | jnp.where(lane == lax.shift_right_logical(ref, 4), bit, 0)
    first, rest = lowest_bit_index(wanted)
    second, rest = lowest_bit_index(rest)
    third, rest = lowest_bit_index(rest)
    table[me] = first + second * 16 + third * 256

    def along_row(k):
        return remote(
            table.at[me], table.at[me], table_send.at[k], table_recv.at[z], ctx=y * COLS + (z + k) % COLS
        )

    def along_row_wait(k):
        origin = (z + COLS - k) % COLS
        ref = table.at[y * COLS + origin]
        remote(ref, ref, table_send.at[k], table_recv.at[origin], ctx=me).wait_recv()

    def rows_of(row):
        return table.at[pl.ds(row * COLS, COLS)]

    def across_rows(k):
        return remote(
            rows_of(y), rows_of(y), table_send.at[COLS + k], table_recv.at[COLS + y],
            ctx=(y + k) % ROWS * COLS + z,
        )

    for k in range(1, COLS):
        along_row(k).start()
    for k in range(1, COLS):
        along_row_wait(k)
    for k in range(1, ROWS):
        across_rows(k).start()
    for k in range(1, ROWS):
        row = (y + ROWS - k) % ROWS
        remote(
            rows_of(row), rows_of(row), table_send.at[COLS + k], table_recv.at[COLS + row], ctx=me
        ).wait_recv()
    for k in range(1, COLS):
        along_row(k).wait_send()
    for k in range(1, ROWS):
        across_rows(k).wait_send()
    to_scalar = pltpu.make_async_copy(table, asked, local_sem.at[2])
    to_scalar.start()
    for k in range(1, HEADS_AX):
        for kv in range(2):
            head_arrival(kv, k).wait_recv()
    for kv in range(2):
        head_copy(kv, 0).wait()
    to_scalar.wait()

    stages = (kstage, vstage)

    def prepare(dr, k, dest):
        packed = asked[dest, 0, me]
        for j in range(CAP):
            block = lax.shift_right_logical(packed, 4 * j) & 15
            for kv in range(2):
                stages[kv][dr, k, pl.ds(j * BLK, BLK), :] = sides[kv][1][block]

    def source(kv, dr, k, dest):
        return stages[kv].at[dr, k]

    exchange(
        1, prepare, source, (krem, vrem), (krelay, vrelay),
        first_send, relay_recv, relay_send, slot_recv,
    )
    for k in range(1, HEADS_AX):
        for kv in range(2):
            head_copy(kv, k).wait_send()


def fetch(lists, key_states, value_states):
    bf16 = jnp.bfloat16
    vmem = pl.BlockSpec(memory_space=pltpu.VMEM)
    anywhere = pl.BlockSpec(memory_space=pl.ANY)
    stage = pltpu.VMEM((ROWS, COLS, SLOT, HEAD_DIM), bf16)
    return pl.pallas_call(
        fetch_kernel,
        in_specs=[pl.BlockSpec(memory_space=pltpu.SMEM), anywhere, anywhere],
        out_specs=[vmem] * 5,
        out_shape=[
            jax.ShapeDtypeStruct((QB, BLK, HEAD_DIM), bf16),
            jax.ShapeDtypeStruct((QB, BLK, HEAD_DIM), bf16),
            jax.ShapeDtypeStruct((REM, HEAD_DIM), bf16),
            jax.ShapeDtypeStruct((REM, HEAD_DIM), bf16),
            jax.ShapeDtypeStruct((CTX, 1, 128), jnp.int32),
        ],
        scratch_shapes=[pltpu.SMEM((CTX, 1, 128), jnp.int32), stage, stage]
        + EXCHANGE_SCRATCH
        + [
            pltpu.SemaphoreType.DMA((2, HEADS_AX)),
            pltpu.SemaphoreType.DMA((2, HEADS_AX)),
            pltpu.SemaphoreType.DMA((COLS + ROWS,)),
            pltpu.SemaphoreType.DMA((COLS + ROWS,)),
            pltpu.SemaphoreType.DMA((3,)),
        ],
        compiler_params=pltpu.CompilerParams(
            collective_id=0, has_side_effects=True, vmem_limit_bytes=14 << 20
        ),
        name="fetch",
    )(lists, key_states, value_states)


def give_back_kernel(
    gkr, gvr, bk, bv, krelay, vrelay, first_send, relay_recv, relay_send, slot_recv
):
    greet(False, True)
    grads = (gkr, gvr)

    def source(kv, dr, k, dest):
        return grads[kv].at[slot_rows(dest)]

    exchange(
        -1, lambda dr, k, dest: None, source, (bk, bv), (krelay, vrelay),
        first_send, relay_recv, relay_send, slot_recv,
    )


def give_back(gkr, gvr):
    vmem = pl.BlockSpec(memory_space=pltpu.VMEM)
    return pl.pallas_call(
        give_back_kernel,
        in_specs=[vmem] * 2,
        out_specs=[vmem] * 2,
        out_shape=[jax.ShapeDtypeStruct((REM, HEAD_DIM), jnp.bfloat16)] * 2,
        scratch_shapes=EXCHANGE_SCRATCH,
        compiler_params=pltpu.CompilerParams(
            collective_id=1, has_side_effects=True, vmem_limit_bytes=14 << 20
        ),
        name="give_back",
    )(gkr, gvr)


def add_up_kernel(asked, gkl, gvl, bk, bv, kout, vout, kacc, vacc):
    me = lax.axis_index("ctx")
    kacc[...] = gkl[...]
    vacc[...] = gvl[...]

    def step(origin, _):
        packed = asked[origin, 0, me]
        for j in range(CAP):
            block = lax.shift_right_logical(packed, 4 * j) & 15
            rows = pl.ds(pl.multiple_of(block * BLK, BLK), BLK)
            came = pl.ds(pl.multiple_of(origin * SLOT + j * BLK, BLK), BLK)
            kacc[rows] += bk[came].astype(jnp.float32)
            vacc[rows] += bv[came].astype(jnp.float32)
        return 0

    lax.fori_loop(me + 1, CTX, step, 0)
    kout[...] = kacc[...].astype(jnp.bfloat16)
    vout[...] = vacc[...].astype(jnp.bfloat16)


def add_up(table, gkl, gvl, bk, bv):
    vmem = pl.BlockSpec(memory_space=pltpu.VMEM)
    return pl.pallas_call(
        add_up_kernel,
        in_specs=[pl.BlockSpec(memory_space=pltpu.SMEM)] + [vmem] * 4,
        out_specs=[vmem] * 2,
        out_shape=[jax.ShapeDtypeStruct((TOK, HEAD_DIM), jnp.bfloat16)] * 2,
        scratch_shapes=[pltpu.VMEM((TOK, HEAD_DIM), jnp.float32)] * 2,
        compiler_params=pltpu.CompilerParams(vmem_limit_bytes=14 << 20),
        name="add_up",
    )(table, gkl, gvl, bk, bv)


def spread_kernel(kg, vg, kout, vout, head_send, head_recv, local_sem):
    head = lax.axis_index("head")
    greet(True, False)
    sides = ((kg, kout), (vg, vout))
    mine = pl.ds(pl.multiple_of(head * HEAD_DIM, HEAD_DIM), HEAD_DIM)

    def copy(kv, k):
        src, dst = sides[kv]
        peer = (head + k) % HEADS_AX
        rows = src.at[pl.ds(pl.multiple_of(peer * HEAD_DIM, HEAD_DIM), HEAD_DIM)]
        if k == 0:
            return pltpu.make_async_copy(rows, dst.at[:, mine], local_sem.at[kv])
        return remote(rows, dst.at[:, mine], head_send.at[kv, k], head_recv.at[kv, head], head=peer)

    def arrival(kv, k):
        peer = (head + HEADS_AX - k) % HEADS_AX
        cols = pl.ds(pl.multiple_of(peer * HEAD_DIM, HEAD_DIM), HEAD_DIM)
        ref = sides[kv][1].at[:, cols]
        return remote(ref, ref, head_send.at[kv, k], head_recv.at[kv, peer], head=head)

    order = (4, 3, 5, 2, 6, 1, 7)
    for k in order:
        for kv in range(2):
            copy(kv, k).start()
    for kv in range(2):
        copy(kv, 0).start()
    for k in order:
        for kv in range(2):
            copy(kv, k).wait_send()
            arrival(kv, k).wait_recv()
    for kv in range(2):
        copy(kv, 0).wait()


def spread(kg, vg):
    vmem = pl.BlockSpec(memory_space=pltpu.VMEM)
    return pl.pallas_call(
        spread_kernel,
        in_specs=[vmem] * 2,
        out_specs=[vmem] * 2,
        out_shape=[jax.ShapeDtypeStruct((TOK // HEADS_AX, HEADS_AX * HEAD_DIM), jnp.bfloat16)] * 2,
        scratch_shapes=[
            pltpu.SemaphoreType.DMA((2, HEADS_AX)),
            pltpu.SemaphoreType.DMA((2, HEADS_AX)),
            pltpu.SemaphoreType.DMA((2,)),
        ],
        compiler_params=pltpu.CompilerParams(
            collective_id=2, has_side_effects=True, vmem_limit_bytes=8 << 20
        ),
        name="spread",
    )(kg, vg)


def per_device(queries, key_states, value_states, block_lists, out_grad):
    by_block = (OWN, BLK, HEADS_AX * HEAD_DIM)
    kloc, vloc, krem, vrem, table = fetch(
        block_lists, key_states.reshape(by_block), value_states.reshape(by_block)
    )
    kloc, vloc = kloc.reshape(TOK, HEAD_DIM), vloc.reshape(TOK, HEAD_DIM)
    att, dq, gkl, gvl, gkr, gvr = attend(
        block_lists, queries, out_grad, kloc, vloc, krem, vrem
    )
    bk, bv = give_back(gkr, gvr)
    kg, vg = add_up(table, gkl, gvl, bk, bv)
    key_grad, value_grad = spread(kg, vg)
    return att, dq, key_grad, value_grad


def solution(mesh):
    return jax.shard_map(
        per_device,
        mesh=mesh,
        in_specs=(
            P("ctx", "head"),
            P(("ctx", "head"), None),
            P(("ctx", "head"), None),
            P("ctx", None),
            P("ctx", "head"),
        ),
        out_specs=(
            P("ctx", "head"),
            P("ctx", "head"),
            P(("ctx", "head"), None),
            P(("ctx", "head"), None),
        ),
        check_vma=False,
    )
```

```python
import functools

import jax
import jax.numpy as jnp
from jax import lax
from jax.experimental import pallas as pl
from jax.experimental.pallas import tpu as pltpu
from jax.sharding import PartitionSpec as P

HEAD_DIM = 128
GROUP = 4
BLK = 64
LIST = 8
CAP = 3
QB = 16
ROWS = 4
COLS = 8
CTX = ROWS * COLS
HEADS_AX = 8
TOK = QB * BLK
SLOT = CAP * BLK
OWN = QB // HEADS_AX
REM = CTX * SLOT
ALL = TOK + REM
NEG_FILL = -1e30
SCALE = HEAD_DIM ** (-0.5)
LOG2E = 1.4426950408889634
STEP = 4

NT = (((1,), (1,)), ((), ()))
TN = (((0,), (0,)), ((), ()))
NN = (((1,), (0,)), ((), ()))


def dot(a, b, dims):
    return lax.dot_general(a, b, dims, preferred_element_type=jnp.float32)


def here():
    me = lax.axis_index("ctx")
    return lax.axis_index("head"), me, me // COLS, me % COLS


def remote(src, dst, send_sem, recv_sem, **device):
    return pltpu.make_async_remote_copy(
        src_ref=src,
        dst_ref=dst,
        send_sem=send_sem,
        recv_sem=recv_sem,
        device_id=device,
        device_id_type=pl.DeviceIdType.MESH,
    )


def greet():
    head, me, y, z = here()
    barrier = pltpu.get_barrier_semaphore()
    peers = [{"head": (head + k) % HEADS_AX} for k in range(1, HEADS_AX)]
    peers += [{"ctx": y * COLS + (z + k) % COLS} for k in range(1, COLS)]
    peers += [{"ctx": (y + k) % ROWS * COLS + z} for k in range(1, ROWS)]
    for peer in peers:
        pl.semaphore_signal(barrier, inc=1, device_id=peer, device_id_type=pl.DeviceIdType.MESH)
    pl.semaphore_wait(barrier, len(peers))


def inside(value, limit):
    return jnp.logical_and(value >= 0, value < limit)


def along_first(dr, odd):
    return dr == 3 or (dr == 2 and odd)


class Exchange:
    def __init__(self, sign, kv, prepare, source, slots, base, relay, sems):
        self.sign, self.kv, self.prepare, self.source = sign, kv, prepare, source
        self.slots, self.base, self.relay = slots, base, relay
        self.first_send, self.relay_recv, self.relay_send, self.slot_recv = sems
        _, self.me, self.y, self.z = here()

    def slot(self, origin):
        return self.slots.at[pl.ds(self.base + origin * CAP, CAP)]

    def dest(self, dr, k):
        return (self.y + self.sign * dr) * COLS + (self.z + self.sign * k + COLS) % COLS

    def copy(self, dr, k, odd):
        src = self.source(dr, k, self.dest(dr, k))
        send = self.first_send.at[self.kv, dr, k]
        if dr == 0 or odd is None:
            return remote(
                src, self.slot(self.me), send, self.slot_recv.at[self.kv, self.me], ctx=self.dest(dr, k)
            )
        col = (self.z + self.sign * k + COLS) % COLS
        row = self.y + self.sign * dr
        target = self.y * COLS + col if along_first(dr, odd) else row * COLS + self.z
        return remote(
            src, self.relay.at[dr - 1, k], send, self.relay_recv.at[self.kv, dr - 1, k], ctx=target
        )

    def sent(self, dr, k):
        if dr == 0:
            return inside(self.z + self.sign * k, COLS)
        return inside(self.y + self.sign * dr, ROWS)

    def start(self, dr, k, odd):
        @pl.when(self.sent(dr, k))
        def _():
            self.prepare(dr, k, self.dest(dr, k))
            self.copy(dr, k, odd).start()

    def each(self, step):
        def odd_step(m, _):
            step(2 * m + 1, True)
            return 0

        def even_step(m, _):
            step(2 * m + 2, False)
            return 0

        lax.fori_loop(0, COLS // 2, odd_step, 0)
        lax.fori_loop(0, COLS // 2 - 1, even_step, 0)

    def send(self):
        def cross(k, odd):
            for dr in (3, 2, 1):
                self.start(dr, k, odd)

        self.each(cross)
        for dr in (3, 2, 1):
            self.start(dr, 0, None)
        self.each(lambda k, odd: self.start(0, k, odd))

    def relayed(self, dr, odd):
        step = self.sign * dr
        return inside(self.y + step if along_first(dr, odd) else self.y - step, ROWS)

    def relay_copy(self, dr, k, odd):
        if along_first(dr, odd):
            origin = self.y * COLS + (self.z - self.sign * k + COLS) % COLS
            target = (self.y + self.sign * dr) * COLS + self.z
        else:
            origin = (self.y - self.sign * dr) * COLS + self.z
            target = self.y * COLS + (self.z + self.sign * k + COLS) % COLS
        return remote(
            self.relay.at[dr - 1, k],
            self.slot(origin),
            self.relay_send.at[self.kv, dr - 1, k],
            self.slot_recv.at[self.kv, origin],
            ctx=target,
        )

    def pass_on(self, k, odd):
        for dr in (3, 2, 1):

            @pl.when(self.relayed(dr, odd))
            def _(dr=dr):
                ref = self.relay.at[dr - 1, k]
                remote(
                    ref, ref, self.relay_send.at[self.kv, dr - 1, k],
                    self.relay_recv.at[self.kv, dr - 1, k], ctx=self.me,
                ).wait_recv()
                self.relay_copy(dr, k, odd).start()

    def arrived(self, origin):
        ref = self.slot(origin)
        remote(
            ref, ref, self.first_send.at[self.kv, 0, 0], self.slot_recv.at[self.kv, origin], ctx=self.me
        ).wait_recv()

    def receive(self):
        def step(k, _):
            @pl.when(inside(self.z - self.sign * k, COLS))
            def _():
                self.arrived(self.y * COLS + self.z - self.sign * k)

            return 0

        lax.fori_loop(1, COLS, step, 0)
        for dr in (1, 2, 3):

            @pl.when(inside(self.y - self.sign * dr, ROWS))
            def _(dr=dr):
                def col(c, _):
                    self.arrived((self.y - self.sign * dr) * COLS + c)
                    return 0

                lax.fori_loop(0, COLS, col, 0)

    def drain(self):
        def step(k, odd):
            for dr in range(ROWS):

                @pl.when(self.sent(dr, k))
                def _(dr=dr):
                    self.copy(dr, k, odd).wait_send()

            for dr in (1, 2, 3):

                @pl.when(self.relayed(dr, odd))
                def _(dr=dr):
                    self.relay_copy(dr, k, odd).wait_send()

        self.each(step)
        for dr in (1, 2, 3):

            @pl.when(self.sent(dr, 0))
            def _(dr=dr):
                self.copy(dr, 0, None).wait_send()


def lowest_bit_index(bits):
    low = bits & (-bits)
    index = jnp.where((low & 0xAAAA) != 0, 1, 0)
    index += jnp.where((low & 0xCCCC) != 0, 2, 0)
    index += jnp.where((low & 0xF0F0) != 0, 4, 0)
    index += jnp.where((low & 0xFF00) != 0, 8, 0)
    return index, bits & (bits - 1)


def as_int(flags):
    return jnp.where(flags, 1, 0)


def down(row):
    return jnp.transpose(jnp.broadcast_to(row, (128, 128)))


def sorted_places(key):
    entry = lax.broadcasted_iota(jnp.int32, (128, 128), 0)
    lane = lax.broadcasted_iota(jnp.int32, (128, 128), 1)
    other = down(key)
    ahead = jnp.logical_and(other == key, entry < lane)
    place = jnp.sum(as_int(jnp.logical_or(other < key, ahead)), axis=0, keepdims=True)
    first = as_int(jnp.sum(as_int(ahead), axis=0, keepdims=True) == 0)
    place_down, first_down = down(place), down(first)
    at = place_down == lane
    order = jnp.sum(jnp.where(at, entry, 0), axis=0, keepdims=True)
    opens = jnp.sum(jnp.where(at, first_down, 0), axis=0, keepdims=True)
    return place_down, first_down, other, order, opens


def last_places(group, place_down):
    lane = lax.broadcasted_iota(jnp.int32, (128, 128), 1)
    return jnp.max(jnp.where(down(group) == lane, place_down, -1), axis=0, keepdims=True)


def reference_tables(me, key):
    place_down, first_down, other, order, opens = sorted_places(key)
    owner = lax.shift_right_logical(key, 4)
    same = jnp.logical_and(lax.shift_right_logical(other, 4) == owner, other < key)
    rank = jnp.sum(jnp.where(same, first_down, 0), axis=0, keepdims=True)
    slot = jnp.where(owner == me, key & 15, QB + owner * CAP + rank)
    return slot, order, opens, last_places(slot, place_down)


def mega_kernel(
    lists, key_in, value_in, q_in, do_in,
    att, dq, kout, vout,
    table, asked, plan, plan_s, back, back_s,
    q3, do3, kloc, vloc, kall, vall, kstage, vstage, krelay, vrelay, kback, vback,
    probs_buf, terms, run, gkl, gvl, gkr, gvr, bk, bv, kg, vg,
    f1, f2, f3, f4, b1, b2, b3, b4,
    head_send, head_recv, out_send, out_recv, table_send, table_recv, local_sem,
):
    head, me, y, z = here()
    loads = [
        pltpu.make_async_copy(q_in, q3, local_sem.at[0]),
        pltpu.make_async_copy(do_in, do3, local_sem.at[1]),
    ]
    for load in loads:
        load.start()
    greet()
    sides = ((key_in, kloc), (value_in, vloc))

    def head_copy(kv, k):
        src, dst = sides[kv]
        peer = (head + k) % HEADS_AX
        cols = pl.ds(pl.multiple_of(peer * HEAD_DIM, HEAD_DIM), HEAD_DIM)
        mine = pl.ds(head * OWN, OWN)
        if k == 0:
            return pltpu.make_async_copy(src.at[:, :, cols], dst.at[mine], local_sem.at[2 + kv])
        return remote(
            src.at[:, :, cols], dst.at[mine], head_send.at[kv, k], head_recv.at[kv, head], head=peer
        )

    def head_arrivals(kv):
        for k in range(1, HEADS_AX):
            peer = (head + HEADS_AX - k) % HEADS_AX
            dst = sides[kv][1].at[pl.ds(peer * OWN, OWN)]
            remote(dst, dst, head_send.at[kv, k], head_recv.at[kv, peer], head=head).wait_recv()
        head_copy(kv, 0).wait()

    for kv in range(2):
        for k in (4, 3, 5, 2, 6, 1, 7, 0):
            head_copy(kv, k).start()

    lane = lax.broadcasted_iota(jnp.int32, (1, 128), 1)
    wanted = jnp.zeros((1, 128), jnp.int32)
    refs = jnp.zeros((1, 128), jnp.int32)
    for i in range(QB):
        for j in range(LIST):
            ref = lists[i, j]
            low, high = ref & 3, lax.shift_right_logical(ref, 2) & 3
            bit = (1 + (low & 1)) * (1 + 3 * lax.shift_right_logical(low, 1))
            bit = bit * (1 + 15 * (high & 1)) * (1 + 255 * lax.shift_right_logical(high, 1))
            wanted = wanted | jnp.where(lane == lax.shift_right_logical(ref, 4), bit, 0)
            refs = jnp.where(lane == i * LIST + j, ref, refs)
    first, rest = lowest_bit_index(wanted)
    second, rest = lowest_bit_index(rest)
    third, rest = lowest_bit_index(rest)
    table[me] = first + second * 16 + third * 256

    def along_row(k):
        return remote(
            table.at[me], table.at[me], table_send.at[k], table_recv.at[z], ctx=y * COLS + (z + k) % COLS
        )

    def rows_of(row):
        return table.at[pl.ds(row * COLS, COLS)]

    def across_rows(k):
        return remote(
            rows_of(y), rows_of(y), table_send.at[COLS + k], table_recv.at[COLS + y],
            ctx=(y + k) % ROWS * COLS + z,
        )

    for k in range(1, COLS):
        along_row(k).start()
    for row, values in enumerate(reference_tables(me, refs)):
        plan[pl.ds(row, 1), :] = values
    plan_copy = pltpu.make_async_copy(plan, plan_s, local_sem.at[4])
    plan_copy.start()
    for k in range(1, COLS):
        origin = (z + COLS - k) % COLS
        ref = table.at[y * COLS + origin]
        remote(ref, ref, table_send.at[k], table_recv.at[origin], ctx=me).wait_recv()
    for k in range(1, ROWS):
        across_rows(k).start()
    for k in range(1, ROWS):
        row = (y + ROWS - k) % ROWS
        remote(
            rows_of(row), rows_of(row), table_send.at[COLS + k], table_recv.at[COLS + row], ctx=me
        ).wait_recv()
    for k in range(1, COLS):
        along_row(k).wait_send()
    for k in range(1, ROWS):
        across_rows(k).wait_send()
    asked_copy = pltpu.make_async_copy(table, asked, local_sem.at[5])
    asked_copy.start()
    asked_copy.wait()

    def stager(stage, local):
        def prepare(dr, k, dest):
            packed = asked[dest, 0, me]
            for j in range(CAP):
                stage[dr, k, j] = local[lax.shift_right_logical(packed, 4 * j) & 15]

        return prepare

    nothing = lambda dr, k, dest: None
    fwd, bwd = (f1, f2, f3, f4), (b1, b2, b3, b4)
    keys_fwd = Exchange(
        1, 0, stager(kstage, kloc), lambda dr, k, dest: kstage.at[dr, k], kall, QB, krelay, fwd
    )
    values_fwd = Exchange(
        1, 1, stager(vstage, vloc), lambda dr, k, dest: vstage.at[dr, k], vall, QB, vrelay, fwd
    )
    keys_back = Exchange(
        -1, 0, nothing, lambda dr, k, dest: gkr.at[pl.ds(dest * CAP, CAP)], bk, 0, kback, bwd
    )
    values_back = Exchange(
        -1, 1, nothing, lambda dr, k, dest: gvr.at[pl.ds(dest * CAP, CAP)], bv, 0, vback, bwd
    )

    head_arrivals(0)
    keys_fwd.send()
    head_arrivals(1)
    values_fwd.send()

    wanted_by = jnp.full((1, 128), QB + 1, jnp.int32)
    for origin in range(CTX):
        packed = asked[origin, 0, me]
        for j in range(CAP):
            block = jnp.where(origin > me, lax.shift_right_logical(packed, 4 * j) & 15, QB)
            wanted_by = jnp.where(lane == origin * CAP + j, block, wanted_by)
    place_down, _, _, order, opens = sorted_places(wanted_by)
    back[pl.ds(0, 1), :] = order
    back[pl.ds(1, 1), :] = opens
    back[pl.ds(2, 1), :] = last_places(wanted_by, place_down)
    back_copy = pltpu.make_async_copy(back, back_s, local_sem.at[6])
    back_copy.start()
    kall[pl.ds(0, QB)] = kloc[...]
    vall[pl.ds(0, QB)] = vloc[...]

    keys_fwd.each(keys_fwd.pass_on)
    for load in loads:
        load.wait()
    plan_copy.wait()
    back_copy.wait()
    keys_fwd.receive()

    key_row = lax.broadcasted_iota(jnp.int32, (BLK, GROUP * BLK), 0)
    query_col = lax.broadcasted_iota(jnp.int32, (BLK, GROUP * BLK), 1) % BLK
    hidden = jnp.where(key_row > query_col, NEG_FILL, 0.0).astype(jnp.float32)

    def heads_of(ref, i):
        return jnp.concatenate(
            [ref[i, :, g * HEAD_DIM : (g + 1) * HEAD_DIM] for g in range(GROUP)], axis=0
        )

    def listed(ref, i):
        return jnp.concatenate([ref[plan_s[0, i * LIST + j]] for j in range(LIST)], axis=0)

    def weigh(i, _):
        do = heads_of(do3, i)
        raw = dot(listed(kall, i), heads_of(q3, i), NT) * (SCALE * LOG2E)
        parts = []
        for j in range(LIST):
            part = raw[j * BLK : (j + 1) * BLK]
            own = jnp.where(lists[i, j] == me * QB + i, 1.0, 0.0)
            parts.append(part + (hidden if j == 0 else hidden * own))
        scores = jnp.concatenate(parts, axis=0)
        expo = jnp.exp2(scores - jnp.max(scores, axis=0, keepdims=True))
        low = (expo * (1.0 / jnp.sum(expo, axis=0, keepdims=True))).astype(jnp.bfloat16)
        probs_buf[i] = low
        terms[pl.ds(i * LIST, LIST)] = dot(low, do, NN).reshape(LIST, BLK, HEAD_DIM)
        return 0

    def differentiate(i, _):
        q, do = heads_of(q3, i), heads_of(do3, i)
        keys, values = listed(kall, i), listed(vall, i)
        low = probs_buf[i]
        probs = low.astype(jnp.float32)
        weighted = probs * dot(values, do, NT)
        delta = jnp.sum(weighted, axis=0, keepdims=True)
        dscore = (weighted - probs * delta).astype(jnp.bfloat16)
        out = jnp.transpose(dot(values, low, TN)).astype(jnp.bfloat16)
        grad = (jnp.transpose(dot(keys, dscore, TN)) * SCALE).astype(jnp.bfloat16)
        for g in range(GROUP):
            att[i, :, g * HEAD_DIM : (g + 1) * HEAD_DIM] = out[g * BLK : (g + 1) * BLK]
            dq[i, :, g * HEAD_DIM : (g + 1) * HEAD_DIM] = grad[g * BLK : (g + 1) * BLK]
        terms[pl.ds(i * LIST, LIST)] = dot(dscore, q, NN).reshape(LIST, BLK, HEAD_DIM)
        return 0

    def running(count, entry, starts, load):
        def step(p, acc):
            acc = jnp.where(starts(p) == 1, 0.0, acc) + load(entry(p))
            run[p] = acc
            return acc

        lax.fori_loop(0, count, step, jnp.zeros((BLK, HEAD_DIM), jnp.float32))

    def total(last):
        return jnp.where(last >= 0, run[jnp.maximum(last, 0)], 0.0)

    def by_slot(local, far, scale):
        running(QB * LIST, lambda p: plan_s[1, p], lambda p: plan_s[2, p], lambda e: terms[e])

        def far_step(e, _):
            far[e] = (total(plan_s[3, QB + e]) * scale).astype(jnp.bfloat16)
            return 0

        lax.fori_loop(0, CAP * me, far_step, 0)

        def local_step(b, _):
            local[b] = total(plan_s[3, b]) * scale
            return 0

        lax.fori_loop(0, QB, local_step, 0)

    def by_block(came, local, out):
        running(
            CAP * (CTX - 1 - me), lambda p: back_s[0, p], lambda p: back_s[1, p],
            lambda e: came[e].astype(jnp.float32),
        )

        def step(b, _):
            out[b] = (local[b] + total(back_s[2, b])).astype(jnp.bfloat16)
            return 0

        lax.fori_loop(0, QB, step, 0)

    outs = ((kg, kout), (vg, vout))

    def out_copy(kv, k):
        src, dst = outs[kv]
        peer = (head + k) % HEADS_AX
        rows = src.at[pl.ds(peer * OWN, OWN)]
        to = dst.at[:, :, pl.ds(pl.multiple_of(head * HEAD_DIM, HEAD_DIM), HEAD_DIM)]
        if k == 0:
            return pltpu.make_async_copy(rows, to, local_sem.at[kv])
        return remote(rows, to, out_send.at[kv, k], out_recv.at[kv, head], head=peer)

    def spread(kv):
        for k in (4, 3, 5, 2, 6, 1, 7, 0):
            out_copy(kv, k).start()

    def gathered(kv):
        for k in range(1, HEADS_AX):
            peer = (head + HEADS_AX - k) % HEADS_AX
            ref = outs[kv][1].at[:, :, pl.ds(pl.multiple_of(peer * HEAD_DIM, HEAD_DIM), HEAD_DIM)]
            remote(ref, ref, out_send.at[kv, k], out_recv.at[kv, peer], head=head).wait_recv()
            out_copy(kv, k).wait_send()
        out_copy(kv, 0).wait()

    def between(exchange, work):
        def odd_step(m, _):
            lax.fori_loop(m * STEP, (m + 1) * STEP, work, 0)
            exchange.pass_on(2 * m + 1, True)
            return 0

        def even_step(m, _):
            exchange.pass_on(2 * m + 2, False)
            return 0

        lax.fori_loop(0, COLS // 2, odd_step, 0)
        return even_step

    even_step = between(values_fwd, weigh)
    by_slot(gvl, gvr, 1.0)
    values_back.send()
    lax.fori_loop(0, COLS // 2 - 1, even_step, 0)
    values_fwd.receive()
    even_step = between(values_back, differentiate)
    by_slot(gkl, gkr, SCALE)
    keys_back.send()
    lax.fori_loop(0, COLS // 2 - 1, even_step, 0)
    keys_back.each(keys_back.pass_on)
    values_back.receive()
    by_block(bv, gvl, vg)
    spread(1)
    keys_back.receive()
    by_block(bk, gkl, kg)
    spread(0)
    for exchange in (keys_fwd, values_fwd, values_back, keys_back):
        exchange.drain()
    for kv in range(2):
        for k in range(1, HEADS_AX):
            head_copy(kv, k).wait_send()
    gathered(1)
    gathered(0)


def per_device(queries, key_states, value_states, block_lists, out_grad):
    bf16, f32, i32 = jnp.bfloat16, jnp.float32, jnp.int32
    wide, full = GROUP * HEAD_DIM, HEADS_AX * HEAD_DIM
    dma = pltpu.SemaphoreType.DMA
    vmem = pl.BlockSpec(memory_space=pltpu.VMEM)
    anywhere = pl.BlockSpec(memory_space=pl.ANY)

    def blocks(n, dtype):
        return pltpu.VMEM((n, BLK, HEAD_DIM), dtype)

    def bundles(rows):
        return pltpu.VMEM((rows, COLS, CAP, BLK, HEAD_DIM), bf16)

    exchange_sems = [
        dma((2, ROWS, COLS)), dma((2, ROWS - 1, COLS)), dma((2, ROWS - 1, COLS)), dma((2, CTX)),
    ]
    far = CTX * CAP
    att, dq, key_grad, value_grad = pl.pallas_call(
        mega_kernel,
        in_specs=[pl.BlockSpec(memory_space=pltpu.SMEM)] + [anywhere] * 4,
        out_specs=[vmem] * 4,
        out_shape=[
            jax.ShapeDtypeStruct((QB, BLK, wide), bf16),
            jax.ShapeDtypeStruct((QB, BLK, wide), bf16),
            jax.ShapeDtypeStruct((OWN, BLK, full), bf16),
            jax.ShapeDtypeStruct((OWN, BLK, full), bf16),
        ],
        scratch_shapes=[
            pltpu.VMEM((CTX, 1, 128), i32), pltpu.SMEM((CTX, 1, 128), i32),
            pltpu.VMEM((8, 128), i32), pltpu.SMEM((8, 128), i32),
            pltpu.VMEM((8, 128), i32), pltpu.SMEM((8, 128), i32),
            pltpu.VMEM((QB, BLK, wide), bf16), pltpu.VMEM((QB, BLK, wide), bf16),
            blocks(QB, bf16), blocks(QB, bf16), blocks(QB + far, bf16), blocks(QB + far, bf16),
            bundles(ROWS), bundles(ROWS),
            bundles(ROWS - 1), bundles(ROWS - 1), bundles(ROWS - 1), bundles(ROWS - 1),
            pltpu.VMEM((QB, LIST * BLK, GROUP * BLK), bf16),
            blocks(QB * LIST, f32), blocks(QB * LIST, f32),
            blocks(QB, f32), blocks(QB, f32), blocks(far, bf16), blocks(far, bf16),
            blocks(far, bf16), blocks(far, bf16), blocks(QB, bf16), blocks(QB, bf16),
        ]
        + exchange_sems
        + exchange_sems
        + [
            dma((2, HEADS_AX)), dma((2, HEADS_AX)), dma((2, HEADS_AX)), dma((2, HEADS_AX)),
            dma((COLS + ROWS,)), dma((COLS + ROWS,)), dma((7,)),
        ],
        compiler_params=pltpu.CompilerParams(
            collective_id=0, has_side_effects=True, vmem_limit_bytes=60 << 20
        ),
        name="mega",
    )(
        block_lists,
        key_states.reshape(OWN, BLK, full),
        value_states.reshape(OWN, BLK, full),
        queries.reshape(QB, BLK, wide),
        out_grad.reshape(QB, BLK, wide),
    )
    return (
        att.reshape(TOK, wide),
        dq.reshape(TOK, wide),
        key_grad.reshape(OWN * BLK, full),
        value_grad.reshape(OWN * BLK, full),
    )


def solution(mesh):
    return jax.shard_map(
        per_device,
        mesh=mesh,
        in_specs=(
            P("ctx", "head"),
            P(("ctx", "head"), None),
            P(("ctx", "head"), None),
            P("ctx", None),
            P("ctx", "head"),
        ),
        out_specs=(
            P("ctx", "head"),
            P("ctx", "head"),
            P(("ctx", "head"), None),
            P(("ctx", "head"), None),
        ),
        check_vma=False,
    )
```

```python
import functools

import jax
import jax.numpy as jnp
from jax import lax
from jax.experimental import pallas as pl
from jax.experimental.pallas import tpu as pltpu
from jax.sharding import PartitionSpec as P

HEAD_DIM = 128
GROUP = 4
BLK = 64
LIST = 8
CAP = 3
QB = 16
ROWS = 4
COLS = 8
CTX = ROWS * COLS
HEADS_AX = 8
TOK = QB * BLK
SLOT = CAP * BLK
OWN = QB // HEADS_AX
REM = CTX * SLOT
ALL = TOK + REM
NEG_FILL = -1e30
SCALE = HEAD_DIM ** (-0.5)
LOG2E = 1.4426950408889634
UNROLL = 2

NT = (((1,), (1,)), ((), ()))
TN = (((0,), (0,)), ((), ()))
NN = (((1,), (0,)), ((), ()))


def dot(a, b, dims):
    return lax.dot_general(a, b, dims, preferred_element_type=jnp.float32)


def here():
    me = lax.axis_index("ctx")
    return lax.axis_index("head"), me, me // COLS, me % COLS


def remote(src, dst, send_sem, recv_sem, **device):
    return pltpu.make_async_remote_copy(
        src_ref=src,
        dst_ref=dst,
        send_sem=send_sem,
        recv_sem=recv_sem,
        device_id=device,
        device_id_type=pl.DeviceIdType.MESH,
    )


def greet():
    head, me, y, z = here()
    barrier = pltpu.get_barrier_semaphore()
    peers = [{"head": (head + k) % HEADS_AX} for k in range(1, HEADS_AX)]
    peers += [{"ctx": y * COLS + (z + k) % COLS} for k in range(1, COLS)]
    peers += [{"ctx": (y + k) % ROWS * COLS + z} for k in range(1, ROWS)]
    for peer in peers:
        pl.semaphore_signal(barrier, inc=1, device_id=peer, device_id_type=pl.DeviceIdType.MESH)
    pl.semaphore_wait(barrier, len(peers))


def inside(value, limit):
    return jnp.logical_and(value >= 0, value < limit)


def along_first(dr, odd):
    return dr == 3 or (dr == 2 and odd)


class Exchange:
    def __init__(self, sign, kv, prepare, source, slots, base, relay, sems):
        self.sign, self.kv, self.prepare, self.source = sign, kv, prepare, source
        self.slots, self.base, self.relay = slots, base, relay
        sems = [sem.at[kv] for sem in sems]
        self.cross_send, self.own_send, self.relay_recv, self.relay_send, self.row_recv, self.own_recv = sems
        _, self.me, self.y, self.z = here()

    def slot(self, origin):
        return self.slots.at[pl.ds(self.base + origin * CAP, CAP)]

    def dest(self, dr, k):
        return (self.y + self.sign * dr) * COLS + (self.z + self.sign * k + COLS) % COLS

    def copy(self, dr, k, odd):
        src = self.source(dr, k, self.dest(dr, k))
        if dr == 0:
            return remote(
                src, self.slot(self.me), self.own_send.at[k], self.own_recv.at[self.z], ctx=self.dest(dr, k)
            )
        send = self.cross_send.at[dr - 1]
        if odd is None:
            return remote(src, self.slot(self.me), send, self.row_recv.at[self.y], ctx=self.dest(dr, k))
        col = (self.z + self.sign * k + COLS) % COLS
        row = self.y + self.sign * dr
        target = self.y * COLS + col if along_first(dr, odd) else row * COLS + self.z
        return remote(
            src, self.relay.at[dr - 1, k], send, self.relay_recv.at[dr - 1, k - 1], ctx=target
        )

    def sent(self, dr, k):
        if dr == 0:
            return inside(self.z + self.sign * k, COLS)
        return inside(self.y + self.sign * dr, ROWS)

    def start(self, dr, k, odd):
        @pl.when(self.sent(dr, k))
        def _():
            self.prepare(dr, k, self.dest(dr, k))
            self.copy(dr, k, odd).start()

    def each(self, step):
        def odd_step(m, _):
            step(2 * m + 1, True)
            return 0

        def even_step(m, _):
            step(2 * m + 2, False)
            return 0

        lax.fori_loop(0, COLS // 2, odd_step, 0)
        lax.fori_loop(0, COLS // 2 - 1, even_step, 0)

    def send(self):
        def cross(k, odd):
            for dr in (3, 2, 1):
                self.start(dr, k, odd)

        self.each(cross)
        for dr in (3, 2, 1):
            self.start(dr, 0, None)
        self.each(lambda k, odd: self.start(0, k, odd))

    def relayed(self, dr, odd):
        step = self.sign * dr
        return inside(self.y + step if along_first(dr, odd) else self.y - step, ROWS)

    def relay_copy(self, dr, k, odd):
        if along_first(dr, odd):
            row, col = self.y, (self.z - self.sign * k + COLS) % COLS
            target = (self.y + self.sign * dr) * COLS + self.z
        else:
            row, col = self.y - self.sign * dr, self.z
            target = self.y * COLS + (self.z + self.sign * k + COLS) % COLS
        return remote(
            self.relay.at[dr - 1, k],
            self.slot(row * COLS + col),
            self.relay_send.at[dr - 1, 1 if odd else 0],
            self.row_recv.at[row],
            ctx=target,
        )

    def pass_on(self, k, odd):
        for dr in (3, 2, 1):

            @pl.when(self.relayed(dr, odd))
            def _(dr=dr):
                self.await_bytes(self.relay.at[dr - 1, k], None, self.relay_recv.at[dr - 1, k - 1])
                self.relay_copy(dr, k, odd).start()

    def await_bytes(self, ref, send, recv):
        if send is None:
            remote(ref, ref, self.own_send.at[0], recv, ctx=self.me).wait_recv()
        else:
            remote(ref, ref, send, self.own_recv.at[0], ctx=self.me).wait_send()

    def receive(self):
        def step(k, _):
            col = self.z - self.sign * k

            @pl.when(inside(col, COLS))
            def _():
                self.await_bytes(self.slot(self.y * COLS + col), None, self.own_recv.at[col])

            return 0

        lax.fori_loop(1, COLS, step, 0)
        for dr in (1, 2, 3):
            row = self.y - self.sign * dr

            @pl.when(inside(row, ROWS))
            def _(row=row):
                ref = self.slots.at[pl.ds(self.base + row * COLS * CAP, COLS * CAP)]
                self.await_bytes(ref, None, self.row_recv.at[row])

    def drain(self):
        def step(k, _):
            @pl.when(self.sent(0, k))
            def _():
                self.copy(0, k, None).wait_send()

            return 0

        lax.fori_loop(1, COLS, step, 0)
        for dr in (1, 2, 3):

            @pl.when(self.sent(dr, 0))
            def _(dr=dr):
                self.await_bytes(self.relay.at[dr - 1], self.cross_send.at[dr - 1], None)

            for odd in (False, True):
                count = COLS // 2 if odd else COLS // 2 - 1

                @pl.when(self.relayed(dr, odd))
                def _(dr=dr, odd=odd, count=count):
                    ref = self.relay.at[dr - 1, pl.ds(0, count)]
                    self.await_bytes(ref, self.relay_send.at[dr - 1, 1 if odd else 0], None)


def lowest_bit_index(bits):
    low = bits & (-bits)
    index = jnp.where((low & 0xAAAA) != 0, 1, 0)
    index += jnp.where((low & 0xCCCC) != 0, 2, 0)
    index += jnp.where((low & 0xF0F0) != 0, 4, 0)
    index += jnp.where((low & 0xFF00) != 0, 8, 0)
    return index, bits & (bits - 1)


def as_int(flags):
    return jnp.where(flags, 1, 0)


def down(row):
    return jnp.transpose(jnp.broadcast_to(row, (128, 128)))


def sorted_places(key):
    entry = lax.broadcasted_iota(jnp.int32, (128, 128), 0)
    lane = lax.broadcasted_iota(jnp.int32, (128, 128), 1)
    other = down(key)
    ahead = jnp.logical_and(other == key, entry < lane)
    place = jnp.sum(as_int(jnp.logical_or(other < key, ahead)), axis=0, keepdims=True)
    first = as_int(jnp.sum(as_int(ahead), axis=0, keepdims=True) == 0)
    place_down, first_down = down(place), down(first)
    at = place_down == lane
    order = jnp.sum(jnp.where(at, entry, 0), axis=0, keepdims=True)
    opens = jnp.sum(jnp.where(at, first_down, 0), axis=0, keepdims=True)
    return place_down, first_down, other, order, opens


def last_places(group, place_down):
    lane = lax.broadcasted_iota(jnp.int32, (128, 128), 1)
    return jnp.max(jnp.where(down(group) == lane, place_down, -1), axis=0, keepdims=True)


def reference_tables(me, key):
    place_down, first_down, other, order, opens = sorted_places(key)
    owner = lax.shift_right_logical(key, 4)
    same = jnp.logical_and(lax.shift_right_logical(other, 4) == owner, other < key)
    rank = jnp.sum(jnp.where(same, first_down, 0), axis=0, keepdims=True)
    slot = jnp.where(owner == me, key & 15, QB + owner * CAP + rank)
    return slot, order, opens, last_places(slot, place_down)


def mega_kernel(
    lists, key_in, value_in, q_in, do_in,
    att, dq, kout, vout,
    table, asked, plan, plan_s, back, back_s,
    q3, do3, kloc, vloc, kall, vall, kstage, vstage, krelay, vrelay, kback, vback,
    probs_buf, terms, run, gkl, gvl, gkr, gvr, bk, bv, kg, vg, kpre, vpre, kland, vland,
    f1, f2, f3, f4, f5, f6, b1, b2, b3, b4, b5, b6,
    head_send, head_recv, out_send, out_recv, table_send, table_recv, local_sem, split_sem,
):
    head, me, y, z = here()
    loads = [
        pltpu.make_async_copy(q_in, q3, local_sem.at[0]),
        pltpu.make_async_copy(do_in, do3, local_sem.at[1]),
    ]
    for load in loads:
        load.start()
    sides = ((key_in, kpre, kloc), (value_in, vpre, vloc))

    def split_copy(kv, peer):
        cols = pl.ds(peer * HEAD_DIM, HEAD_DIM)
        return pltpu.make_async_copy(
            sides[kv][0].at[:, :, cols], sides[kv][1].at[peer], split_sem.at[kv]
        )

    def head_copy(kv, k):
        _, src, dst = sides[kv]
        peer = (head + k) % HEADS_AX
        mine = pl.ds(head * OWN, OWN)
        if k == 0:
            return pltpu.make_async_copy(src.at[peer], dst.at[mine], local_sem.at[2 + kv])
        return remote(
            src.at[peer], dst.at[mine], head_send.at[kv], head_recv.at[kv], head=peer
        )

    def head_wait(kv):
        ref = sides[kv][2].at[pl.ds(0, (HEADS_AX - 1) * OWN)]
        return remote(ref, ref, head_send.at[kv], head_recv.at[kv], head=head)

    def head_arrivals(kv):
        head_wait(kv).wait_recv()
        head_copy(kv, 0).wait()

    for kv in range(2):
        for peer in range(HEADS_AX):
            split_copy(kv, peer).start()

    lane = lax.broadcasted_iota(jnp.int32, (1, 128), 1)
    wanted = jnp.zeros((1, 128), jnp.int32)
    refs = jnp.zeros((1, 128), jnp.int32)
    for i in range(QB):
        for j in range(LIST):
            ref = lists[i, j]
            low, high = ref & 3, lax.shift_right_logical(ref, 2) & 3
            bit = (1 + (low & 1)) * (1 + 3 * lax.shift_right_logical(low, 1))
            bit = bit * (1 + 15 * (high & 1)) * (1 + 255 * lax.shift_right_logical(high, 1))
            wanted = wanted | jnp.where(lane == lax.shift_right_logical(ref, 4), bit, 0)
            refs = jnp.where(lane == i * LIST + j, ref, refs)
    first, rest = lowest_bit_index(wanted)
    second, rest = lowest_bit_index(rest)
    third, rest = lowest_bit_index(rest)
    table[me] = first + second * 16 + third * 256
    for kv in range(2):
        whole = sides[kv][1]
        pltpu.make_async_copy(whole, whole, split_sem.at[kv]).wait()
    greet()

    def along_row(k):
        return remote(
            table.at[me], table.at[me], table_send.at[0], table_recv.at[0], ctx=y * COLS + (z + k) % COLS
        )

    def rows_of(row):
        return table.at[pl.ds(row * COLS, COLS)]

    def across_rows(k):
        return remote(
            rows_of(y), rows_of(y), table_send.at[1], table_recv.at[1],
            ctx=(y + k) % ROWS * COLS + z,
        )

    for k in range(1, COLS):
        along_row(k).start()
    for kv in range(2):
        for k in (4, 3, 5, 2, 6, 1, 7, 0):
            head_copy(kv, k).start()
    for row, values in enumerate(reference_tables(me, refs)):
        plan[pl.ds(row, 1), :] = values
    plan_copy = pltpu.make_async_copy(plan, plan_s, local_sem.at[4])
    plan_copy.start()
    def table_wait(phase, rows):
        ref = table.at[pl.ds(0, rows)]
        return remote(ref, ref, table_send.at[phase], table_recv.at[phase], ctx=me)

    table_wait(0, COLS - 1).wait_recv()
    for k in range(1, ROWS):
        across_rows(k).start()
    table_wait(1, CTX - COLS).wait_recv()
    table_wait(0, COLS - 1).wait_send()
    table_wait(1, CTX - COLS).wait_send()
    asked_copy = pltpu.make_async_copy(table, asked, local_sem.at[5])
    asked_copy.start()
    asked_copy.wait()

    def stager(stage, local):
        def prepare(dr, k, dest):
            packed = asked[dest, 0, me]
            for j in range(CAP):
                stage[dr, k, j] = local[lax.shift_right_logical(packed, 4 * j) & 15]

        return prepare

    nothing = lambda dr, k, dest: None
    fwd, bwd = (f1, f2, f3, f4, f5, f6), (b1, b2, b3, b4, b5, b6)
    keys_fwd = Exchange(
        1, 0, stager(kstage, kloc), lambda dr, k, dest: kstage.at[dr, k], kall, QB, krelay, fwd
    )
    values_fwd = Exchange(
        1, 1, stager(vstage, vloc), lambda dr, k, dest: vstage.at[dr, k], vall, QB, vrelay, fwd
    )
    keys_back = Exchange(
        -1, 0, nothing, lambda dr, k, dest: gkr.at[pl.ds(dest * CAP, CAP)], bk, 0, kback, bwd
    )
    values_back = Exchange(
        -1, 1, nothing, lambda dr, k, dest: gvr.at[pl.ds(dest * CAP, CAP)], bv, 0, vback, bwd
    )

    head_arrivals(0)
    keys_fwd.send()
    head_arrivals(1)
    values_fwd.send()

    wanted_by = jnp.full((1, 128), QB + 1, jnp.int32)
    for origin in range(CTX):
        packed = asked[origin, 0, me]
        for j in range(CAP):
            block = jnp.where(origin > me, lax.shift_right_logical(packed, 4 * j) & 15, QB)
            wanted_by = jnp.where(lane == origin * CAP + j, block, wanted_by)
    place_down, _, _, order, opens = sorted_places(wanted_by)
    back[pl.ds(0, 1), :] = order
    back[pl.ds(1, 1), :] = opens
    back[pl.ds(2, 1), :] = last_places(wanted_by, place_down)
    back_copy = pltpu.make_async_copy(back, back_s, local_sem.at[6])
    back_copy.start()
    kall[pl.ds(0, QB)] = kloc[...]
    vall[pl.ds(0, QB)] = vloc[...]

    keys_fwd.each(keys_fwd.pass_on)
    for load in loads:
        load.wait()
    plan_copy.wait()
    back_copy.wait()
    keys_fwd.receive()

    key_row = lax.broadcasted_iota(jnp.int32, (BLK, GROUP * BLK), 0)
    query_col = lax.broadcasted_iota(jnp.int32, (BLK, GROUP * BLK), 1) % BLK
    hidden = jnp.where(key_row > query_col, NEG_FILL, 0.0).astype(jnp.float32)

    def heads_of(ref, i):
        return jnp.concatenate(
            [ref[i, :, g * HEAD_DIM : (g + 1) * HEAD_DIM] for g in range(GROUP)], axis=0
        )

    def listed(ref, i):
        return jnp.concatenate([ref[plan_s[0, i * LIST + j]] for j in range(LIST)], axis=0)

    def weigh(i, _):
        do = heads_of(do3, i)
        raw = dot(listed(kall, i), heads_of(q3, i), NT) * (SCALE * LOG2E)
        parts = []
        for j in range(LIST):
            part = raw[j * BLK : (j + 1) * BLK]
            own = jnp.where(lists[i, j] == me * QB + i, 1.0, 0.0)
            parts.append(part + (hidden if j == 0 else hidden * own))
        scores = jnp.concatenate(parts, axis=0)
        expo = jnp.exp2(scores - jnp.max(scores, axis=0, keepdims=True))
        low = (expo * (1.0 / jnp.sum(expo, axis=0, keepdims=True))).astype(jnp.bfloat16)
        probs_buf[i] = low
        terms[pl.ds(i * LIST, LIST)] = dot(low, do, NN).reshape(LIST, BLK, HEAD_DIM)
        return 0

    def differentiate(i, _):
        q, do = heads_of(q3, i), heads_of(do3, i)
        keys, values = listed(kall, i), listed(vall, i)
        low = probs_buf[i]
        probs = low.astype(jnp.float32)
        weighted = probs * dot(values, do, NT)
        delta = jnp.sum(weighted, axis=0, keepdims=True)
        dscore = (weighted - probs * delta).astype(jnp.bfloat16)
        out = jnp.transpose(dot(values, low, TN)).astype(jnp.bfloat16)
        grad = (jnp.transpose(dot(keys, dscore, TN)) * SCALE).astype(jnp.bfloat16)
        for g in range(GROUP):
            att[i, :, g * HEAD_DIM : (g + 1) * HEAD_DIM] = out[g * BLK : (g + 1) * BLK]
            dq[i, :, g * HEAD_DIM : (g + 1) * HEAD_DIM] = grad[g * BLK : (g + 1) * BLK]
        terms[pl.ds(i * LIST, LIST)] = dot(dscore, q, NN).reshape(LIST, BLK, HEAD_DIM)
        return 0

    def running(count, entry, starts, load):
        def step(p, acc):
            acc = jnp.where(starts(p) == 1, 0.0, acc) + load(entry(p))
            run[p] = acc
            return acc

        lax.fori_loop(0, count, step, jnp.zeros((BLK, HEAD_DIM), jnp.float32))

    def total(last):
        return jnp.where(last >= 0, run[jnp.maximum(last, 0)], 0.0)

    def by_slot(local, far, scale):
        running(QB * LIST, lambda p: plan_s[1, p], lambda p: plan_s[2, p], lambda e: terms[e])

        def far_step(e, _):
            far[e] = (total(plan_s[3, QB + e]) * scale).astype(jnp.bfloat16)
            return 0

        lax.fori_loop(0, CAP * me, far_step, 0)

        def local_step(b, _):
            local[b] = total(plan_s[3, b]) * scale
            return 0

        lax.fori_loop(0, QB, local_step, 0)

    def by_block(came, local, out):
        running(
            CAP * (CTX - 1 - me), lambda p: back_s[0, p], lambda p: back_s[1, p],
            lambda e: came[e].astype(jnp.float32),
        )

        def step(b, _):
            out[b] = (local[b] + total(back_s[2, b])).astype(jnp.bfloat16)
            return 0

        lax.fori_loop(0, QB, step, 0)

    outs = ((kg, kland, kout), (vg, vland, vout))

    def out_copy(kv, k):
        src, land, _ = outs[kv]
        peer = (head + k) % HEADS_AX
        return remote(
            src.at[pl.ds(peer * OWN, OWN)], land.at[head], out_send.at[kv], out_recv.at[kv], head=peer
        )

    def spread(kv):
        for k in (4, 3, 5, 2, 6, 1, 7):
            out_copy(kv, k).start()
        src, land, _ = outs[kv]
        land[head] = src[pl.ds(head * OWN, OWN)]

    def gathered(kv):
        _, land, out = outs[kv]
        ref = land.at[pl.ds(0, HEADS_AX - 1)]
        wait = remote(ref, ref, out_send.at[kv], out_recv.at[kv], head=head)
        wait.wait_recv()
        for peer in range(HEADS_AX):
            out[:, :, peer * HEAD_DIM : (peer + 1) * HEAD_DIM] = land[peer]
        wait.wait_send()

    def between(exchange, work):
        order = [(k, True) for k in (1, 3, 5, 7)] + [(k, False) for k in (2, 4, 6)]
        for part in range(QB // UNROLL):
            for u in range(UNROLL):
                work(part * UNROLL + u, 0)
            if part >= 1:
                exchange.pass_on(*order[part - 1])


    between(values_fwd, weigh)
    by_slot(gvl, gvr, 1.0)
    values_back.send()
    values_fwd.receive()
    between(values_back, differentiate)
    by_slot(gkl, gkr, SCALE)
    keys_back.send()
    keys_back.each(keys_back.pass_on)
    values_back.receive()
    by_block(bv, gvl, vg)
    spread(1)
    keys_back.receive()
    by_block(bk, gkl, kg)
    spread(0)
    for exchange in (keys_fwd, values_fwd, values_back, keys_back):
        exchange.drain()
    for kv in range(2):
        head_wait(kv).wait_send()
    gathered(1)
    gathered(0)


def per_device(queries, key_states, value_states, block_lists, out_grad):
    bf16, f32, i32 = jnp.bfloat16, jnp.float32, jnp.int32
    wide, full = GROUP * HEAD_DIM, HEADS_AX * HEAD_DIM
    dma = pltpu.SemaphoreType.DMA
    vmem = pl.BlockSpec(memory_space=pltpu.VMEM)
    anywhere = pl.BlockSpec(memory_space=pl.ANY)

    def blocks(n, dtype):
        return pltpu.VMEM((n, BLK, HEAD_DIM), dtype)

    def bundles(rows):
        return pltpu.VMEM((rows, COLS, CAP, BLK, HEAD_DIM), bf16)

    exchange_sems = [
        dma((2, ROWS - 1)), dma((2, COLS)), dma((2, ROWS - 1, COLS - 1)), dma((2, ROWS - 1, 2)),
        dma((2, ROWS)), dma((2, COLS)),
    ]
    far = CTX * CAP
    att, dq, key_grad, value_grad = pl.pallas_call(
        mega_kernel,
        in_specs=[pl.BlockSpec(memory_space=pltpu.SMEM)] + [anywhere] * 4,
        out_specs=[vmem] * 4,
        out_shape=[
            jax.ShapeDtypeStruct((QB, BLK, wide), bf16),
            jax.ShapeDtypeStruct((QB, BLK, wide), bf16),
            jax.ShapeDtypeStruct((OWN, BLK, full), bf16),
            jax.ShapeDtypeStruct((OWN, BLK, full), bf16),
        ],
        scratch_shapes=[
            pltpu.VMEM((CTX, 1, 128), i32), pltpu.SMEM((CTX, 1, 128), i32),
            pltpu.VMEM((8, 128), i32), pltpu.SMEM((8, 128), i32),
            pltpu.VMEM((8, 128), i32), pltpu.SMEM((8, 128), i32),
            pltpu.VMEM((QB, BLK, wide), bf16), pltpu.VMEM((QB, BLK, wide), bf16),
            blocks(QB, bf16), blocks(QB, bf16), blocks(QB + far, bf16), blocks(QB + far, bf16),
            bundles(ROWS), bundles(ROWS),
            bundles(ROWS - 1), bundles(ROWS - 1), bundles(ROWS - 1), bundles(ROWS - 1),
            pltpu.VMEM((QB, LIST * BLK, GROUP * BLK), bf16),
            blocks(QB * LIST, f32), blocks(QB * LIST, f32),
            blocks(QB, f32), blocks(QB, f32), blocks(far, bf16), blocks(far, bf16),
            blocks(far, bf16), blocks(far, bf16), blocks(QB, bf16), blocks(QB, bf16),
        ]
        + [pltpu.VMEM((HEADS_AX, OWN, BLK, HEAD_DIM), bf16)] * 4
        + exchange_sems
        + exchange_sems
        + [
            dma((2,)), dma((2,)), dma((2,)), dma((2,)), dma((2,)), dma((2,)), dma((7,)), dma((2,)),
        ],
        compiler_params=pltpu.CompilerParams(
            collective_id=0, has_side_effects=True, vmem_limit_bytes=60 << 20
        ),
        name="mega",
    )(
        block_lists,
        key_states.reshape(OWN, BLK, full),
        value_states.reshape(OWN, BLK, full),
        queries.reshape(QB, BLK, wide),
        out_grad.reshape(QB, BLK, wide),
    )
    return (
        att.reshape(TOK, wide),
        dq.reshape(TOK, wide),
        key_grad.reshape(OWN * BLK, full),
        value_grad.reshape(OWN * BLK, full),
    )


def solution(mesh):
    return jax.shard_map(
        per_device,
        mesh=mesh,
        in_specs=(
            P("ctx", "head"),
            P(("ctx", "head"), None),
            P(("ctx", "head"), None),
            P("ctx", None),
            P("ctx", "head"),
        ),
        out_specs=(
            P("ctx", "head"),
            P("ctx", "head"),
            P(("ctx", "head"), None),
            P(("ctx", "head"), None),
        ),
        check_vma=False,
    )
```

```python
import functools

import jax
import jax.numpy as jnp
from jax import lax
from jax.experimental import pallas as pl
from jax.experimental.pallas import tpu as pltpu
from jax.sharding import PartitionSpec as P

HEAD_DIM = 128
GROUP = 4
BLK = 64
LIST = 8
CAP = 3
QB = 16
ROWS = 4
COLS = 8
CTX = ROWS * COLS
HEADS_AX = 8
TOK = QB * BLK
SLOT = CAP * BLK
OWN = QB // HEADS_AX
REM = CTX * SLOT
ALL = TOK + REM
NEG_FILL = -1e30
SCALE = HEAD_DIM ** (-0.5)
LOG2E = 1.4426950408889634
UNROLL = 2
WEIGH_RELAYS = ((1, 3), (5, 7), (2, 4), (6,), (), (), (), ())
BEFORE_SEND = ()
AFTER_SEND = ()
DIFF_RELAYS = ((1, 3), (5, 7), (2, 4), (6,), (), (), (), ())
BACK_BEFORE = ()
BACK_AFTER = ()

NT = (((1,), (1,)), ((), ()))
TN = (((0,), (0,)), ((), ()))
NN = (((1,), (0,)), ((), ()))


def dot(a, b, dims):
    return lax.dot_general(a, b, dims, preferred_element_type=jnp.float32)


def here():
    me = lax.axis_index("ctx")
    return lax.axis_index("head"), me, me // COLS, me % COLS


def remote(src, dst, send_sem, recv_sem, **device):
    return pltpu.make_async_remote_copy(
        src_ref=src,
        dst_ref=dst,
        send_sem=send_sem,
        recv_sem=recv_sem,
        device_id=device,
        device_id_type=pl.DeviceIdType.MESH,
    )


def greet():
    head, me, y, z = here()
    barrier = pltpu.get_barrier_semaphore()
    peers = [{"head": (head + k) % HEADS_AX} for k in range(1, HEADS_AX)]
    peers += [{"ctx": y * COLS + (z + k) % COLS} for k in range(1, COLS)]
    peers += [{"ctx": (y + k) % ROWS * COLS + z} for k in range(1, ROWS)]
    for peer in peers:
        pl.semaphore_signal(barrier, inc=1, device_id=peer, device_id_type=pl.DeviceIdType.MESH)
    pl.semaphore_wait(barrier, len(peers))


def inside(value, limit):
    return jnp.logical_and(value >= 0, value < limit)


def along_first(dr, odd):
    return dr == 3 or (dr == 2 and odd)


class Exchange:
    def __init__(self, sign, kv, prepare, source, slots, base, relay, sems):
        self.sign, self.kv, self.prepare, self.source = sign, kv, prepare, source
        self.slots, self.base, self.relay = slots, base, relay
        sems = [sem.at[kv] for sem in sems]
        self.cross_send, self.own_send, self.relay_recv, self.relay_send, self.row_recv, self.own_recv = sems
        _, self.me, self.y, self.z = here()

    def slot(self, origin):
        return self.slots.at[pl.ds(self.base + origin * CAP, CAP)]

    def dest(self, dr, k):
        return (self.y + self.sign * dr) * COLS + (self.z + self.sign * k + COLS) % COLS

    def copy(self, dr, k, odd):
        src = self.source(dr, k, self.dest(dr, k))
        if dr == 0:
            return remote(
                src, self.slot(self.me), self.own_send.at[k], self.own_recv.at[self.z], ctx=self.dest(dr, k)
            )
        send = self.cross_send.at[dr - 1]
        if odd is None:
            return remote(src, self.slot(self.me), send, self.row_recv.at[self.y], ctx=self.dest(dr, k))
        col = (self.z + self.sign * k + COLS) % COLS
        row = self.y + self.sign * dr
        target = self.y * COLS + col if along_first(dr, odd) else row * COLS + self.z
        return remote(
            src, self.relay.at[dr - 1, k], send, self.relay_recv.at[dr - 1, k - 1], ctx=target
        )

    def sent(self, dr, k):
        if dr == 0:
            return inside(self.z + self.sign * k, COLS)
        return inside(self.y + self.sign * dr, ROWS)

    def start(self, dr, k, odd):
        @pl.when(self.sent(dr, k))
        def _():
            self.prepare(dr, k, self.dest(dr, k))
            self.copy(dr, k, odd).start()

    def each(self, step):
        def odd_step(m, _):
            step(2 * m + 1, True)
            return 0

        def even_step(m, _):
            step(2 * m + 2, False)
            return 0

        lax.fori_loop(0, COLS // 2, odd_step, 0)
        lax.fori_loop(0, COLS // 2 - 1, even_step, 0)

    def send(self):
        def cross(k, odd):
            for dr in (3, 2, 1):
                self.start(dr, k, odd)

        self.each(cross)
        for dr in (3, 2, 1):
            self.start(dr, 0, None)
        self.each(lambda k, odd: self.start(0, k, odd))

    def relayed(self, dr, odd):
        step = self.sign * dr
        return inside(self.y + step if along_first(dr, odd) else self.y - step, ROWS)

    def relay_copy(self, dr, k, odd):
        if along_first(dr, odd):
            row, col = self.y, (self.z - self.sign * k + COLS) % COLS
            target = (self.y + self.sign * dr) * COLS + self.z
        else:
            row, col = self.y - self.sign * dr, self.z
            target = self.y * COLS + (self.z + self.sign * k + COLS) % COLS
        return remote(
            self.relay.at[dr - 1, k],
            self.slot(row * COLS + col),
            self.relay_send.at[dr - 1, 1 if odd else 0],
            self.row_recv.at[row],
            ctx=target,
        )

    def pass_on(self, k, odd):
        for dr in (3, 2, 1):

            @pl.when(self.relayed(dr, odd))
            def _(dr=dr):
                self.await_bytes(self.relay.at[dr - 1, k], None, self.relay_recv.at[dr - 1, k - 1])
                self.relay_copy(dr, k, odd).start()

    def await_bytes(self, ref, send, recv):
        if send is None:
            remote(ref, ref, self.own_send.at[0], recv, ctx=self.me).wait_recv()
        else:
            remote(ref, ref, send, self.own_recv.at[0], ctx=self.me).wait_send()

    def receive(self):
        def step(k, _):
            col = self.z - self.sign * k

            @pl.when(inside(col, COLS))
            def _():
                self.await_bytes(self.slot(self.y * COLS + col), None, self.own_recv.at[col])

            return 0

        lax.fori_loop(1, COLS, step, 0)
        for dr in (1, 2, 3):
            row = self.y - self.sign * dr

            @pl.when(inside(row, ROWS))
            def _(row=row):
                ref = self.slots.at[pl.ds(self.base + row * COLS * CAP, COLS * CAP)]
                self.await_bytes(ref, None, self.row_recv.at[row])

    def drain(self):
        def step(k, _):
            @pl.when(self.sent(0, k))
            def _():
                self.copy(0, k, None).wait_send()

            return 0

        lax.fori_loop(1, COLS, step, 0)
        for dr in (1, 2, 3):

            @pl.when(self.sent(dr, 0))
            def _(dr=dr):
                self.await_bytes(self.relay.at[dr - 1], self.cross_send.at[dr - 1], None)

            for odd in (False, True):
                count = COLS // 2 if odd else COLS // 2 - 1

                @pl.when(self.relayed(dr, odd))
                def _(dr=dr, odd=odd, count=count):
                    ref = self.relay.at[dr - 1, pl.ds(0, count)]
                    self.await_bytes(ref, self.relay_send.at[dr - 1, 1 if odd else 0], None)


def lowest_bit_index(bits):
    low = bits & (-bits)
    index = jnp.where((low & 0xAAAA) != 0, 1, 0)
    index += jnp.where((low & 0xCCCC) != 0, 2, 0)
    index += jnp.where((low & 0xF0F0) != 0, 4, 0)
    index += jnp.where((low & 0xFF00) != 0, 8, 0)
    return index, bits & (bits - 1)


def as_int(flags):
    return jnp.where(flags, 1, 0)


def down(row):
    return jnp.transpose(jnp.broadcast_to(row, (128, 128)))


def sorted_places(key):
    entry = lax.broadcasted_iota(jnp.int32, (128, 128), 0)
    lane = lax.broadcasted_iota(jnp.int32, (128, 128), 1)
    other = down(key)
    ahead = jnp.logical_and(other == key, entry < lane)
    place = jnp.sum(as_int(jnp.logical_or(other < key, ahead)), axis=0, keepdims=True)
    first = as_int(jnp.sum(as_int(ahead), axis=0, keepdims=True) == 0)
    place_down, first_down = down(place), down(first)
    at = place_down == lane
    order = jnp.sum(jnp.where(at, entry, 0), axis=0, keepdims=True)
    opens = jnp.sum(jnp.where(at, first_down, 0), axis=0, keepdims=True)
    return place_down, first_down, other, order, opens


def last_places(group, place_down):
    lane = lax.broadcasted_iota(jnp.int32, (128, 128), 1)
    return jnp.max(jnp.where(down(group) == lane, place_down, -1), axis=0, keepdims=True)


def reference_tables(me, key):
    place_down, first_down, other, order, opens = sorted_places(key)
    owner = lax.shift_right_logical(key, 4)
    same = jnp.logical_and(lax.shift_right_logical(other, 4) == owner, other < key)
    rank = jnp.sum(jnp.where(same, first_down, 0), axis=0, keepdims=True)
    slot = jnp.where(owner == me, key & 15, QB + owner * CAP + rank)
    return slot, order, opens, last_places(slot, place_down)


def mega_kernel(
    lists, key_in, value_in, q_in, do_in,
    att, dq, kout, vout,
    table, asked, plan, plan_s, back, back_s,
    q3, do3, kloc, vloc, kall, vall, kstage, vstage, krelay, vrelay, kback, vback,
    probs_buf, terms, run, gkl, gvl, gkr, gvr, bk, bv, kg, vg, kpre, vpre, kland, vland,
    f1, f2, f3, f4, f5, f6, b1, b2, b3, b4, b5, b6,
    head_send, head_recv, out_send, out_recv, table_send, table_recv, local_sem, split_sem,
):
    head, me, y, z = here()
    loads = [
        pltpu.make_async_copy(q_in, q3, local_sem.at[0]),
        pltpu.make_async_copy(do_in, do3, local_sem.at[1]),
    ]
    for load in loads:
        load.start()
    sides = ((key_in, kpre, kloc), (value_in, vpre, vloc))

    def split_copy(kv, peer):
        cols = pl.ds(peer * HEAD_DIM, HEAD_DIM)
        return pltpu.make_async_copy(
            sides[kv][0].at[:, :, cols], sides[kv][1].at[peer], split_sem.at[kv]
        )

    def head_copy(kv, k):
        _, src, dst = sides[kv]
        peer = (head + k) % HEADS_AX
        mine = pl.ds(head * OWN, OWN)
        if k == 0:
            return pltpu.make_async_copy(src.at[peer], dst.at[mine], local_sem.at[2 + kv])
        return remote(
            src.at[peer], dst.at[mine], head_send.at[kv], head_recv.at[kv], head=peer
        )

    def head_wait(kv):
        ref = sides[kv][2].at[pl.ds(0, (HEADS_AX - 1) * OWN)]
        return remote(ref, ref, head_send.at[kv], head_recv.at[kv], head=head)

    def head_arrivals(kv):
        head_wait(kv).wait_recv()
        head_copy(kv, 0).wait()

    for kv in range(2):
        for peer in range(HEADS_AX):
            split_copy(kv, peer).start()

    lane = lax.broadcasted_iota(jnp.int32, (1, 128), 1)
    wanted = jnp.zeros((1, 128), jnp.int32)
    refs = jnp.zeros((1, 128), jnp.int32)
    for i in range(QB):
        for j in range(LIST):
            ref = lists[j, i]
            low, high = ref & 3, lax.shift_right_logical(ref, 2) & 3
            bit = (1 + (low & 1)) * (1 + 3 * lax.shift_right_logical(low, 1))
            bit = bit * (1 + 15 * (high & 1)) * (1 + 255 * lax.shift_right_logical(high, 1))
            wanted = wanted | jnp.where(lane == lax.shift_right_logical(ref, 4), bit, 0)
            refs = jnp.where(lane == i * LIST + j, ref, refs)
    first, rest = lowest_bit_index(wanted)
    second, rest = lowest_bit_index(rest)
    third, rest = lowest_bit_index(rest)
    table[me] = first + second * 16 + third * 256
    for kv in range(2):
        whole = sides[kv][1]
        pltpu.make_async_copy(whole, whole, split_sem.at[kv]).wait()
    greet()

    def along_row(k):
        return remote(
            table.at[me], table.at[me], table_send.at[0], table_recv.at[0], ctx=y * COLS + (z + k) % COLS
        )

    def rows_of(row):
        return table.at[pl.ds(row * COLS, COLS)]

    def across_rows(k):
        return remote(
            rows_of(y), rows_of(y), table_send.at[1], table_recv.at[1],
            ctx=(y + k) % ROWS * COLS + z,
        )

    for k in range(1, COLS):
        along_row(k).start()
    for kv in range(2):
        for k in (4, 3, 5, 2, 6, 1, 7, 0):
            head_copy(kv, k).start()
    for row, values in enumerate(reference_tables(me, refs)):
        plan[pl.ds(row, 1), :] = values
    plan_copy = pltpu.make_async_copy(plan, plan_s, local_sem.at[4])
    plan_copy.start()
    def table_wait(phase, rows):
        ref = table.at[pl.ds(0, rows)]
        return remote(ref, ref, table_send.at[phase], table_recv.at[phase], ctx=me)

    table_wait(0, COLS - 1).wait_recv()
    for k in range(1, ROWS):
        across_rows(k).start()
    table_wait(1, CTX - COLS).wait_recv()
    table_wait(0, COLS - 1).wait_send()
    table_wait(1, CTX - COLS).wait_send()
    asked_copy = pltpu.make_async_copy(table, asked, local_sem.at[5])
    asked_copy.start()
    asked_copy.wait()

    def stager(stage, local):
        def prepare(dr, k, dest):
            packed = asked[dest, 0, me]
            for j in range(CAP):
                stage[dr, k, j] = local[lax.shift_right_logical(packed, 4 * j) & 15]

        return prepare

    nothing = lambda dr, k, dest: None
    fwd, bwd = (f1, f2, f3, f4, f5, f6), (b1, b2, b3, b4, b5, b6)
    keys_fwd = Exchange(
        1, 0, stager(kstage, kloc), lambda dr, k, dest: kstage.at[dr, k], kall, QB, krelay, fwd
    )
    values_fwd = Exchange(
        1, 1, stager(vstage, vloc), lambda dr, k, dest: vstage.at[dr, k], vall, QB, vrelay, fwd
    )
    keys_back = Exchange(
        -1, 0, nothing, lambda dr, k, dest: gkr.at[pl.ds(dest * CAP, CAP)], bk, 0, kback, bwd
    )
    values_back = Exchange(
        -1, 1, nothing, lambda dr, k, dest: gvr.at[pl.ds(dest * CAP, CAP)], bv, 0, vback, bwd
    )

    head_arrivals(0)
    keys_fwd.send()
    head_arrivals(1)
    values_fwd.send()

    wanted_by = jnp.full((1, 128), QB + 1, jnp.int32)
    for origin in range(CTX):
        packed = asked[origin, 0, me]
        for j in range(CAP):
            block = jnp.where(origin > me, lax.shift_right_logical(packed, 4 * j) & 15, QB)
            wanted_by = jnp.where(lane == origin * CAP + j, block, wanted_by)
    place_down, _, _, order, opens = sorted_places(wanted_by)
    back[pl.ds(0, 1), :] = order
    back[pl.ds(1, 1), :] = opens
    back[pl.ds(2, 1), :] = last_places(wanted_by, place_down)
    back_copy = pltpu.make_async_copy(back, back_s, local_sem.at[6])
    back_copy.start()
    kall[pl.ds(0, QB)] = kloc[...]
    vall[pl.ds(0, QB)] = vloc[...]

    keys_fwd.each(keys_fwd.pass_on)
    for load in loads:
        load.wait()
    plan_copy.wait()
    back_copy.wait()
    keys_fwd.receive()

    key_row = lax.broadcasted_iota(jnp.int32, (BLK, GROUP * BLK), 0)
    query_col = lax.broadcasted_iota(jnp.int32, (BLK, GROUP * BLK), 1) % BLK
    hidden = jnp.where(key_row > query_col, NEG_FILL, 0.0).astype(jnp.float32)

    def heads_of(ref, i):
        return jnp.concatenate(
            [ref[i, :, g * HEAD_DIM : (g + 1) * HEAD_DIM] for g in range(GROUP)], axis=0
        )

    def listed(ref, i):
        return jnp.concatenate([ref[plan_s[0, i * LIST + j]] for j in range(LIST)], axis=0)

    def weigh(i, _):
        do = heads_of(do3, i)
        raw = dot(listed(kall, i), heads_of(q3, i), NT) * (SCALE * LOG2E)
        parts = []
        for j in range(LIST):
            part = raw[j * BLK : (j + 1) * BLK]
            own = jnp.where(lists[j, i] == me * QB + i, 1.0, 0.0)
            parts.append(part + (hidden if j == 0 else hidden * own))
        scores = jnp.concatenate(parts, axis=0)
        expo = jnp.exp2(scores - jnp.max(scores, axis=0, keepdims=True))
        low = (expo * (1.0 / jnp.sum(expo, axis=0, keepdims=True))).astype(jnp.bfloat16)
        probs_buf[i] = low
        terms[pl.ds(i * LIST, LIST)] = dot(low, do, NN).reshape(LIST, BLK, HEAD_DIM)
        return 0

    def differentiate(i, _):
        q, do = heads_of(q3, i), heads_of(do3, i)
        keys, values = listed(kall, i), listed(vall, i)
        low = probs_buf[i]
        probs = low.astype(jnp.float32)
        weighted = probs * dot(values, do, NT)
        delta = jnp.sum(weighted, axis=0, keepdims=True)
        dscore = (weighted - probs * delta).astype(jnp.bfloat16)
        out = jnp.transpose(dot(values, low, TN)).astype(jnp.bfloat16)
        grad = (jnp.transpose(dot(keys, dscore, TN)) * SCALE).astype(jnp.bfloat16)
        for g in range(GROUP):
            att[i, :, g * HEAD_DIM : (g + 1) * HEAD_DIM] = out[g * BLK : (g + 1) * BLK]
            dq[i, :, g * HEAD_DIM : (g + 1) * HEAD_DIM] = grad[g * BLK : (g + 1) * BLK]
        terms[pl.ds(i * LIST, LIST)] = dot(dscore, q, NN).reshape(LIST, BLK, HEAD_DIM)
        return 0

    def running(count, entry, starts, load):
        def step(p, acc):
            acc = jnp.where(starts(p) == 1, 0.0, acc) + load(entry(p))
            run[p] = acc
            return acc

        lax.fori_loop(0, count, step, jnp.zeros((BLK, HEAD_DIM), jnp.float32))

    def total(last):
        return jnp.where(last >= 0, run[jnp.maximum(last, 0)], 0.0)

    def by_slot(local, far, scale):
        running(QB * LIST, lambda p: plan_s[1, p], lambda p: plan_s[2, p], lambda e: terms[e])

        def far_step(e, _):
            far[e] = (total(plan_s[3, QB + e]) * scale).astype(jnp.bfloat16)
            return 0

        lax.fori_loop(0, CAP * me, far_step, 0)

        def local_step(b, _):
            local[b] = total(plan_s[3, b]) * scale
            return 0

        lax.fori_loop(0, QB, local_step, 0)

    def by_block(came, local, out):
        running(
            CAP * (CTX - 1 - me), lambda p: back_s[0, p], lambda p: back_s[1, p],
            lambda e: came[e].astype(jnp.float32),
        )

        def step(b, _):
            out[b] = (local[b] + total(back_s[2, b])).astype(jnp.bfloat16)
            return 0

        lax.fori_loop(0, QB, step, 0)

    outs = ((kg, kland, kout), (vg, vland, vout))

    def out_copy(kv, k):
        src, land, _ = outs[kv]
        peer = (head + k) % HEADS_AX
        return remote(
            src.at[pl.ds(peer * OWN, OWN)], land.at[head], out_send.at[kv], out_recv.at[kv], head=peer
        )

    def spread(kv):
        for k in (4, 3, 5, 2, 6, 1, 7):
            out_copy(kv, k).start()
        src, land, _ = outs[kv]
        land[head] = src[pl.ds(head * OWN, OWN)]

    def gathered(kv):
        _, land, out = outs[kv]
        ref = land.at[pl.ds(0, HEADS_AX - 1)]
        wait = remote(ref, ref, out_send.at[kv], out_recv.at[kv], head=head)
        wait.wait_recv()
        for peer in range(HEADS_AX):
            out[:, :, peer * HEAD_DIM : (peer + 1) * HEAD_DIM] = land[peer]
        wait.wait_send()

    def between(exchange, work, relays):
        for part in range(QB // UNROLL):
            for u in range(UNROLL):
                work(part * UNROLL + u, 0)
            for k in relays[part]:
                exchange.pass_on(k, k % 2 == 1)

    between(values_fwd, weigh, WEIGH_RELAYS)
    by_slot(gvl, gvr, 1.0)
    for k in BEFORE_SEND:
        values_fwd.pass_on(k, k % 2 == 1)
    values_back.send()
    for k in AFTER_SEND:
        values_fwd.pass_on(k, k % 2 == 1)
    values_fwd.receive()
    between(values_back, differentiate, DIFF_RELAYS)
    by_slot(gkl, gkr, SCALE)
    for k in BACK_BEFORE:
        values_back.pass_on(k, k % 2 == 1)
    keys_back.send()
    for k in BACK_AFTER:
        values_back.pass_on(k, k % 2 == 1)
    keys_back.each(keys_back.pass_on)
    values_back.receive()
    by_block(bv, gvl, vg)
    spread(1)
    keys_back.receive()
    by_block(bk, gkl, kg)
    spread(0)
    for exchange in (keys_fwd, values_fwd, values_back, keys_back):
        exchange.drain()
    for kv in range(2):
        head_wait(kv).wait_send()
    gathered(1)
    gathered(0)


def land_kernel(a, b, c, d, ao, bo, co, do):
    ao[...] = a[...]
    bo[...] = b[...]
    co[...] = c[...]
    do[...] = d[...]


def land(*arrays):
    steps = 4
    specs = []
    for x in arrays:
        rows = x.shape[0] // steps
        specs.append(pl.BlockSpec((rows, x.shape[1]), lambda i: (i, 0)))
    return pl.pallas_call(
        land_kernel,
        grid=(steps,),
        in_specs=specs,
        out_specs=specs,
        out_shape=[jax.ShapeDtypeStruct(x.shape, x.dtype) for x in arrays],
        compiler_params=pltpu.CompilerParams(vmem_limit_bytes=60 << 20),
        name="land",
    )(*arrays)


def per_device(queries, key_states, value_states, block_lists, out_grad):
    bf16, f32, i32 = jnp.bfloat16, jnp.float32, jnp.int32
    wide, full = GROUP * HEAD_DIM, HEADS_AX * HEAD_DIM
    dma = pltpu.SemaphoreType.DMA
    vmem = pl.BlockSpec(memory_space=pltpu.VMEM)
    anywhere = pl.BlockSpec(memory_space=pl.ANY)

    def blocks(n, dtype):
        return pltpu.VMEM((n, BLK, HEAD_DIM), dtype)

    def bundles(rows):
        return pltpu.VMEM((rows, COLS, CAP, BLK, HEAD_DIM), bf16)

    exchange_sems = [
        dma((2, ROWS - 1)), dma((2, COLS)), dma((2, ROWS - 1, COLS - 1)), dma((2, ROWS - 1, 2)),
        dma((2, ROWS)), dma((2, COLS)),
    ]
    far = CTX * CAP
    att, dq, key_grad, value_grad = pl.pallas_call(
        mega_kernel,
        in_specs=[pl.BlockSpec(memory_space=pltpu.SMEM)] + [anywhere] * 4,
        out_specs=[vmem] * 4,
        out_shape=[
            jax.ShapeDtypeStruct((QB, BLK, wide), bf16),
            jax.ShapeDtypeStruct((QB, BLK, wide), bf16),
            jax.ShapeDtypeStruct((OWN, BLK, full), bf16),
            jax.ShapeDtypeStruct((OWN, BLK, full), bf16),
        ],
        scratch_shapes=[
            pltpu.VMEM((CTX, 1, 128), i32), pltpu.SMEM((CTX, 1, 128), i32),
            pltpu.VMEM((8, 128), i32), pltpu.SMEM((8, 128), i32),
            pltpu.VMEM((8, 128), i32), pltpu.SMEM((8, 128), i32),
            pltpu.VMEM((QB, BLK, wide), bf16), pltpu.VMEM((QB, BLK, wide), bf16),
            blocks(QB, bf16), blocks(QB, bf16), blocks(QB + far, bf16), blocks(QB + far, bf16),
            bundles(ROWS), bundles(ROWS),
            bundles(ROWS - 1), bundles(ROWS - 1), bundles(ROWS - 1), bundles(ROWS - 1),
            pltpu.VMEM((QB, LIST * BLK, GROUP * BLK), bf16),
            blocks(QB * LIST, f32), blocks(QB * LIST, f32),
            blocks(QB, f32), blocks(QB, f32), blocks(far, bf16), blocks(far, bf16),
            blocks(far, bf16), blocks(far, bf16), blocks(QB, bf16), blocks(QB, bf16),
        ]
        + [pltpu.VMEM((HEADS_AX, OWN, BLK, HEAD_DIM), bf16)] * 4
        + exchange_sems
        + exchange_sems
        + [
            dma((2,)), dma((2,)), dma((2,)), dma((2,)), dma((2,)), dma((2,)), dma((7,)), dma((2,)),
        ],
        compiler_params=pltpu.CompilerParams(
            collective_id=0, has_side_effects=True, vmem_limit_bytes=60 << 20
        ),
        name="mega",
    )(
        block_lists.T,
        key_states.reshape(OWN, BLK, full),
        value_states.reshape(OWN, BLK, full),
        queries.reshape(QB, BLK, wide),
        out_grad.reshape(QB, BLK, wide),
    )
    return land(
        att.reshape(TOK, wide),
        dq.reshape(TOK, wide),
        key_grad.reshape(OWN * BLK, full),
        value_grad.reshape(OWN * BLK, full),
    )


def solution(mesh):
    return jax.shard_map(
        per_device,
        mesh=mesh,
        in_specs=(
            P("ctx", "head"),
            P(("ctx", "head"), None),
            P(("ctx", "head"), None),
            P("ctx", None),
            P("ctx", "head"),
        ),
        out_specs=(
            P("ctx", "head"),
            P("ctx", "head"),
            P(("ctx", "head"), None),
            P(("ctx", "head"), None),
        ),
        check_vma=False,
    )
```

```python
import functools

import jax
import jax.numpy as jnp
from jax import lax
from jax.experimental import pallas as pl
from jax.experimental.pallas import tpu as pltpu
from jax.sharding import PartitionSpec as P

HEAD_DIM = 128
GROUP = 4
BLK = 64
LIST = 8
CAP = 3
QB = 16
ROWS = 4
COLS = 8
CTX = ROWS * COLS
HEADS_AX = 8
TOK = QB * BLK
SLOT = CAP * BLK
OWN = QB // HEADS_AX
REM = CTX * SLOT
ALL = TOK + REM
NEG_FILL = -1e30
SCALE = HEAD_DIM ** (-0.5)
LOG2E = 1.4426950408889634
UNROLL = 2
WEIGH_RELAYS = ((1, 3), (5, 7), (2, 4), (6,), (), (), (), ())
BEFORE_SEND = ()
AFTER_SEND = ()
DIFF_RELAYS = ((1, 3), (5, 7), (2, 4), (6,), (), (), (), ())
BACK_BEFORE = ()
BACK_AFTER = ()

NT = (((1,), (1,)), ((), ()))
TN = (((0,), (0,)), ((), ()))
NN = (((1,), (0,)), ((), ()))


def dot(a, b, dims):
    return lax.dot_general(a, b, dims, preferred_element_type=jnp.float32)


def here():
    me = lax.axis_index("ctx")
    return lax.axis_index("head"), me, me // COLS, me % COLS


def remote(src, dst, send_sem, recv_sem, **device):
    return pltpu.make_async_remote_copy(
        src_ref=src,
        dst_ref=dst,
        send_sem=send_sem,
        recv_sem=recv_sem,
        device_id=device,
        device_id_type=pl.DeviceIdType.MESH,
    )


def greet():
    head, me, y, z = here()
    barrier = pltpu.get_barrier_semaphore()
    peers = [{"head": (head + k) % HEADS_AX} for k in range(1, HEADS_AX)]
    peers += [{"ctx": y * COLS + (z + k) % COLS} for k in range(1, COLS)]
    peers += [{"ctx": (y + k) % ROWS * COLS + z} for k in range(1, ROWS)]
    for peer in peers:
        pl.semaphore_signal(barrier, inc=1, device_id=peer, device_id_type=pl.DeviceIdType.MESH)
    pl.semaphore_wait(barrier, len(peers))


def inside(value, limit):
    return jnp.logical_and(value >= 0, value < limit)


def along_first(dr, odd):
    return dr == 3 or (dr == 2 and odd)


class Exchange:
    def __init__(self, sign, kv, prepare, source, slots, base, relay, sems):
        self.sign, self.kv, self.prepare, self.source = sign, kv, prepare, source
        self.slots, self.base, self.relay = slots, base, relay
        sems = [sem.at[kv] for sem in sems]
        self.cross_send, self.own_send, self.relay_recv, self.relay_send, self.row_recv, self.own_recv = sems
        _, self.me, self.y, self.z = here()

    def slot(self, origin):
        return self.slots.at[pl.ds(self.base + origin * CAP, CAP)]

    def dest(self, dr, k):
        return (self.y + self.sign * dr) * COLS + (self.z + self.sign * k + COLS) % COLS

    def copy(self, dr, k, odd):
        src = self.source(dr, k, self.dest(dr, k))
        if dr == 0:
            return remote(
                src, self.slot(self.me), self.own_send.at[k], self.own_recv.at[self.z], ctx=self.dest(dr, k)
            )
        send = self.cross_send.at[dr - 1]
        if odd is None:
            return remote(src, self.slot(self.me), send, self.row_recv.at[self.y], ctx=self.dest(dr, k))
        col = (self.z + self.sign * k + COLS) % COLS
        row = self.y + self.sign * dr
        target = self.y * COLS + col if along_first(dr, odd) else row * COLS + self.z
        return remote(
            src, self.relay.at[dr - 1, k], send, self.relay_recv.at[dr - 1, k - 1], ctx=target
        )

    def sent(self, dr, k):
        if dr == 0:
            return inside(self.z + self.sign * k, COLS)
        return inside(self.y + self.sign * dr, ROWS)

    def start(self, dr, k, odd):
        @pl.when(self.sent(dr, k))
        def _():
            self.prepare(dr, k, self.dest(dr, k))
            self.copy(dr, k, odd).start()

    def each(self, step):
        def odd_step(m, _):
            step(2 * m + 1, True)
            return 0

        def even_step(m, _):
            step(2 * m + 2, False)
            return 0

        lax.fori_loop(0, COLS // 2, odd_step, 0)
        lax.fori_loop(0, COLS // 2 - 1, even_step, 0)

    def send(self):
        def cross(k, odd):
            for dr in (3, 2, 1):
                self.start(dr, k, odd)

        self.each(cross)
        for dr in (3, 2, 1):
            self.start(dr, 0, None)
        self.each(lambda k, odd: self.start(0, k, odd))

    def relayed(self, dr, odd):
        step = self.sign * dr
        return inside(self.y + step if along_first(dr, odd) else self.y - step, ROWS)

    def relay_copy(self, dr, k, odd):
        if along_first(dr, odd):
            row, col = self.y, (self.z - self.sign * k + COLS) % COLS
            target = (self.y + self.sign * dr) * COLS + self.z
        else:
            row, col = self.y - self.sign * dr, self.z
            target = self.y * COLS + (self.z + self.sign * k + COLS) % COLS
        return remote(
            self.relay.at[dr - 1, k],
            self.slot(row * COLS + col),
            self.relay_send.at[dr - 1, 1 if odd else 0],
            self.row_recv.at[row],
            ctx=target,
        )

    def pass_on(self, k, odd):
        for dr in (3, 2, 1):

            @pl.when(self.relayed(dr, odd))
            def _(dr=dr):
                self.await_bytes(self.relay.at[dr - 1, k], None, self.relay_recv.at[dr - 1, k - 1])
                self.relay_copy(dr, k, odd).start()

    def await_bytes(self, ref, send, recv):
        if send is None:
            remote(ref, ref, self.own_send.at[0], recv, ctx=self.me).wait_recv()
        else:
            remote(ref, ref, send, self.own_recv.at[0], ctx=self.me).wait_send()

    def receive(self):
        def step(k, _):
            col = self.z - self.sign * k

            @pl.when(inside(col, COLS))
            def _():
                self.await_bytes(self.slot(self.y * COLS + col), None, self.own_recv.at[col])

            return 0

        lax.fori_loop(1, COLS, step, 0)
        for dr in (1, 2, 3):
            row = self.y - self.sign * dr

            @pl.when(inside(row, ROWS))
            def _(row=row):
                ref = self.slots.at[pl.ds(self.base + row * COLS * CAP, COLS * CAP)]
                self.await_bytes(ref, None, self.row_recv.at[row])

    def drain(self):
        def step(k, _):
            @pl.when(self.sent(0, k))
            def _():
                self.copy(0, k, None).wait_send()

            return 0

        lax.fori_loop(1, COLS, step, 0)
        for dr in (1, 2, 3):

            @pl.when(self.sent(dr, 0))
            def _(dr=dr):
                self.await_bytes(self.relay.at[dr - 1], self.cross_send.at[dr - 1], None)

            for odd in (False, True):
                count = COLS // 2 if odd else COLS // 2 - 1

                @pl.when(self.relayed(dr, odd))
                def _(dr=dr, odd=odd, count=count):
                    ref = self.relay.at[dr - 1, pl.ds(0, count)]
                    self.await_bytes(ref, self.relay_send.at[dr - 1, 1 if odd else 0], None)


def lowest_bit_index(bits):
    low = bits & (-bits)
    index = jnp.where((low & 0xAAAA) != 0, 1, 0)
    index += jnp.where((low & 0xCCCC) != 0, 2, 0)
    index += jnp.where((low & 0xF0F0) != 0, 4, 0)
    index += jnp.where((low & 0xFF00) != 0, 8, 0)
    return index, bits & (bits - 1)


def as_int(flags):
    return jnp.where(flags, 1, 0)


def down(row):
    return jnp.transpose(jnp.broadcast_to(row, (128, 128)))


def sorted_places(key):
    entry = lax.broadcasted_iota(jnp.int32, (128, 128), 0)
    lane = lax.broadcasted_iota(jnp.int32, (128, 128), 1)
    other = down(key)
    ahead = jnp.logical_and(other == key, entry < lane)
    place = jnp.sum(as_int(jnp.logical_or(other < key, ahead)), axis=0, keepdims=True)
    first = as_int(jnp.sum(as_int(ahead), axis=0, keepdims=True) == 0)
    place_down, first_down = down(place), down(first)
    at = place_down == lane
    order = jnp.sum(jnp.where(at, entry, 0), axis=0, keepdims=True)
    opens = jnp.sum(jnp.where(at, first_down, 0), axis=0, keepdims=True)
    return place_down, first_down, other, order, opens


def last_places(group, place_down):
    lane = lax.broadcasted_iota(jnp.int32, (128, 128), 1)
    return jnp.max(jnp.where(down(group) == lane, place_down, -1), axis=0, keepdims=True)


def reference_tables(me, key):
    place_down, first_down, other, order, opens = sorted_places(key)
    owner = lax.shift_right_logical(key, 4)
    same = jnp.logical_and(lax.shift_right_logical(other, 4) == owner, other < key)
    rank = jnp.sum(jnp.where(same, first_down, 0), axis=0, keepdims=True)
    slot = jnp.where(owner == me, key & 15, QB + owner * CAP + rank)
    return slot, order, opens, last_places(slot, place_down)


def mega_kernel(
    lists, key_in, value_in, q_in, do_in,
    att_out, dq_out, kout, vout,
    table, asked, plan, plan_s, back, back_s,
    q3, do3, kloc, vloc, kall, vall, kstage, vstage, krelay, vrelay, kback, vback,
    probs_buf, terms, run, gkl, gvl, gkr, gvr, bk, bv, kg, vg, kpre, vpre, kland, vland, att, dq,
    f1, f2, f3, f4, f5, f6, b1, b2, b3, b4, b5, b6,
    head_send, head_recv, out_send, out_recv, table_send, table_recv, local_sem, split_sem,
):
    head, me, y, z = here()
    loads = [
        pltpu.make_async_copy(q_in, q3, local_sem.at[0]),
        pltpu.make_async_copy(do_in, do3, local_sem.at[1]),
    ]
    for load in loads:
        load.start()
    sides = ((key_in, kpre, kloc), (value_in, vpre, vloc))

    def split_copy(kv, peer):
        cols = pl.ds(peer * HEAD_DIM, HEAD_DIM)
        return pltpu.make_async_copy(
            sides[kv][0].at[:, :, cols], sides[kv][1].at[peer], split_sem.at[kv]
        )

    def head_copy(kv, k):
        _, src, dst = sides[kv]
        peer = (head + k) % HEADS_AX
        mine = pl.ds(head * OWN, OWN)
        if k == 0:
            return pltpu.make_async_copy(src.at[peer], dst.at[mine], local_sem.at[2 + kv])
        return remote(
            src.at[peer], dst.at[mine], head_send.at[kv], head_recv.at[kv], head=peer
        )

    def head_wait(kv):
        ref = sides[kv][2].at[pl.ds(0, (HEADS_AX - 1) * OWN)]
        return remote(ref, ref, head_send.at[kv], head_recv.at[kv], head=head)

    def head_arrivals(kv):
        head_wait(kv).wait_recv()
        head_copy(kv, 0).wait()

    for kv in range(2):
        for peer in range(HEADS_AX):
            split_copy(kv, peer).start()

    lane = lax.broadcasted_iota(jnp.int32, (1, 128), 1)
    wanted = jnp.zeros((1, 128), jnp.int32)
    refs = jnp.zeros((1, 128), jnp.int32)
    for i in range(QB):
        for j in range(LIST):
            ref = lists[j, i]
            low, high = ref & 3, lax.shift_right_logical(ref, 2) & 3
            bit = (1 + (low & 1)) * (1 + 3 * lax.shift_right_logical(low, 1))
            bit = bit * (1 + 15 * (high & 1)) * (1 + 255 * lax.shift_right_logical(high, 1))
            wanted = wanted | jnp.where(lane == lax.shift_right_logical(ref, 4), bit, 0)
            refs = jnp.where(lane == i * LIST + j, ref, refs)
    first, rest = lowest_bit_index(wanted)
    second, rest = lowest_bit_index(rest)
    third, rest = lowest_bit_index(rest)
    table[me] = first + second * 16 + third * 256
    for kv in range(2):
        whole = sides[kv][1]
        pltpu.make_async_copy(whole, whole, split_sem.at[kv]).wait()
    greet()

    def along_row(k):
        return remote(
            table.at[me], table.at[me], table_send.at[0], table_recv.at[0], ctx=y * COLS + (z + k) % COLS
        )

    def rows_of(row):
        return table.at[pl.ds(row * COLS, COLS)]

    def across_rows(k):
        return remote(
            rows_of(y), rows_of(y), table_send.at[1], table_recv.at[1],
            ctx=(y + k) % ROWS * COLS + z,
        )

    for k in range(1, COLS):
        along_row(k).start()
    for kv in range(2):
        for k in (4, 3, 5, 2, 6, 1, 7, 0):
            head_copy(kv, k).start()
    for row, values in enumerate(reference_tables(me, refs)):
        plan[pl.ds(row, 1), :] = values
    plan_copy = pltpu.make_async_copy(plan, plan_s, local_sem.at[4])
    plan_copy.start()
    def table_wait(phase, rows):
        ref = table.at[pl.ds(0, rows)]
        return remote(ref, ref, table_send.at[phase], table_recv.at[phase], ctx=me)

    table_wait(0, COLS - 1).wait_recv()
    for k in range(1, ROWS):
        across_rows(k).start()
    table_wait(1, CTX - COLS).wait_recv()
    table_wait(0, COLS - 1).wait_send()
    table_wait(1, CTX - COLS).wait_send()
    asked_copy = pltpu.make_async_copy(table, asked, local_sem.at[5])
    asked_copy.start()
    asked_copy.wait()

    def stager(stage, local):
        def prepare(dr, k, dest):
            packed = asked[dest, 0, me]
            for j in range(CAP):
                stage[dr, k, j] = local[lax.shift_right_logical(packed, 4 * j) & 15]

        return prepare

    nothing = lambda dr, k, dest: None
    fwd, bwd = (f1, f2, f3, f4, f5, f6), (b1, b2, b3, b4, b5, b6)
    keys_fwd = Exchange(
        1, 0, stager(kstage, kloc), lambda dr, k, dest: kstage.at[dr, k], kall, QB, krelay, fwd
    )
    values_fwd = Exchange(
        1, 1, stager(vstage, vloc), lambda dr, k, dest: vstage.at[dr, k], vall, QB, vrelay, fwd
    )
    keys_back = Exchange(
        -1, 0, nothing, lambda dr, k, dest: gkr.at[pl.ds(dest * CAP, CAP)], bk, 0, kback, bwd
    )
    values_back = Exchange(
        -1, 1, nothing, lambda dr, k, dest: gvr.at[pl.ds(dest * CAP, CAP)], bv, 0, vback, bwd
    )

    head_arrivals(0)
    keys_fwd.send()
    head_arrivals(1)
    values_fwd.send()

    wanted_by = jnp.full((1, 128), QB + 1, jnp.int32)
    for origin in range(CTX):
        packed = asked[origin, 0, me]
        for j in range(CAP):
            block = jnp.where(origin > me, lax.shift_right_logical(packed, 4 * j) & 15, QB)
            wanted_by = jnp.where(lane == origin * CAP + j, block, wanted_by)
    place_down, _, _, order, opens = sorted_places(wanted_by)
    back[pl.ds(0, 1), :] = order
    back[pl.ds(1, 1), :] = opens
    back[pl.ds(2, 1), :] = last_places(wanted_by, place_down)
    back_copy = pltpu.make_async_copy(back, back_s, local_sem.at[6])
    back_copy.start()
    kall[pl.ds(0, QB)] = kloc[...]
    vall[pl.ds(0, QB)] = vloc[...]

    keys_fwd.each(keys_fwd.pass_on)
    for load in loads:
        load.wait()
    plan_copy.wait()
    back_copy.wait()
    keys_fwd.receive()

    key_row = lax.broadcasted_iota(jnp.int32, (BLK, GROUP * BLK), 0)
    query_col = lax.broadcasted_iota(jnp.int32, (BLK, GROUP * BLK), 1) % BLK
    hidden = jnp.where(key_row > query_col, NEG_FILL, 0.0).astype(jnp.float32)

    def heads_of(ref, i):
        return jnp.concatenate(
            [ref[i, :, g * HEAD_DIM : (g + 1) * HEAD_DIM] for g in range(GROUP)], axis=0
        )

    def listed(ref, i):
        return jnp.concatenate([ref[plan_s[0, i * LIST + j]] for j in range(LIST)], axis=0)

    def weigh(i, _):
        do = heads_of(do3, i)
        raw = dot(listed(kall, i), heads_of(q3, i), NT) * (SCALE * LOG2E)
        parts = []
        for j in range(LIST):
            part = raw[j * BLK : (j + 1) * BLK]
            own = jnp.where(lists[j, i] == me * QB + i, 1.0, 0.0)
            parts.append(part + (hidden if j == 0 else hidden * own))
        scores = jnp.concatenate(parts, axis=0)
        expo = jnp.exp2(scores - jnp.max(scores, axis=0, keepdims=True))
        low = (expo * (1.0 / jnp.sum(expo, axis=0, keepdims=True))).astype(jnp.bfloat16)
        probs_buf[i] = low
        terms[pl.ds(i * LIST, LIST)] = dot(low, do, NN).reshape(LIST, BLK, HEAD_DIM)
        return 0

    def differentiate(i, _):
        q, do = heads_of(q3, i), heads_of(do3, i)
        keys, values = listed(kall, i), listed(vall, i)
        low = probs_buf[i]
        probs = low.astype(jnp.float32)
        weighted = probs * dot(values, do, NT)
        delta = jnp.sum(weighted, axis=0, keepdims=True)
        dscore = (weighted - probs * delta).astype(jnp.bfloat16)
        out = jnp.transpose(dot(values, low, TN)).astype(jnp.bfloat16)
        grad = (jnp.transpose(dot(keys, dscore, TN)) * SCALE).astype(jnp.bfloat16)
        for g in range(GROUP):
            att[i, :, g * HEAD_DIM : (g + 1) * HEAD_DIM] = out[g * BLK : (g + 1) * BLK]
            dq[i, :, g * HEAD_DIM : (g + 1) * HEAD_DIM] = grad[g * BLK : (g + 1) * BLK]
        terms[pl.ds(i * LIST, LIST)] = dot(dscore, q, NN).reshape(LIST, BLK, HEAD_DIM)
        return 0

    def running(count, width, order_of, load):
        table_s, row = order_of

        def step(m, acc):
            for u in range(width):
                p = m * width + u
                acc = jnp.where(table_s[row + 1, p] == 1, 0.0, acc) + load(table_s[row, p])
                run[p] = acc
            return acc

        lax.fori_loop(0, count, step, jnp.zeros((BLK, HEAD_DIM), jnp.float32))

    def total(last):
        return jnp.where(last >= 0, run[jnp.maximum(last, 0)], 0.0)

    def by_slot(local, far, scale):
        running(QB, LIST, (plan_s, 1), lambda e: terms[e])

        def far_step(owner, _):
            for j in range(CAP):
                e = owner * CAP + j
                far[e] = (total(plan_s[3, QB + e]) * scale).astype(jnp.bfloat16)
            return 0

        lax.fori_loop(0, me, far_step, 0)
        for b in range(QB):
            local[b] = total(plan_s[3, b]) * scale

    def by_block(came, local, out):
        running(CTX - 1 - me, CAP, (back_s, 0), lambda e: came[e].astype(jnp.float32))
        for b in range(QB):
            out[b] = (local[b] + total(back_s[2, b])).astype(jnp.bfloat16)

    outs = ((kg, kland, kout), (vg, vland, vout))

    def out_copy(kv, k):
        src, land, _ = outs[kv]
        peer = (head + k) % HEADS_AX
        return remote(
            src.at[pl.ds(peer * OWN, OWN)], land.at[head], out_send.at[kv], out_recv.at[kv], head=peer
        )

    def spread(kv):
        for k in (4, 3, 5, 2, 6, 1, 7):
            out_copy(kv, k).start()
        src, land, _ = outs[kv]
        land[head] = src[pl.ds(head * OWN, OWN)]

    def gathered(kv):
        _, land, out = outs[kv]
        ref = land.at[pl.ds(0, HEADS_AX - 1)]
        wait = remote(ref, ref, out_send.at[kv], out_recv.at[kv], head=head)
        wait.wait_recv()
        for peer in range(HEADS_AX):
            out[:, :, peer * HEAD_DIM : (peer + 1) * HEAD_DIM] = land[peer]
        wait.wait_send()

    def between(exchange, work, relays):
        for part in range(QB // UNROLL):
            for u in range(UNROLL):
                work(part * UNROLL + u, 0)
            for k in relays[part]:
                exchange.pass_on(k, k % 2 == 1)

    between(values_fwd, weigh, WEIGH_RELAYS)
    by_slot(gvl, gvr, 1.0)
    for k in BEFORE_SEND:
        values_fwd.pass_on(k, k % 2 == 1)
    values_back.send()
    for k in AFTER_SEND:
        values_fwd.pass_on(k, k % 2 == 1)
    values_fwd.receive()
    between(values_back, differentiate, DIFF_RELAYS)
    stores = [
        pltpu.make_async_copy(att, att_out, local_sem.at[0]),
        pltpu.make_async_copy(dq, dq_out, local_sem.at[1]),
    ]
    for store in stores:
        store.start()
    by_slot(gkl, gkr, SCALE)
    for k in BACK_BEFORE:
        values_back.pass_on(k, k % 2 == 1)
    keys_back.send()
    for k in BACK_AFTER:
        values_back.pass_on(k, k % 2 == 1)
    keys_back.each(keys_back.pass_on)
    values_back.receive()
    by_block(bv, gvl, vg)
    spread(1)
    keys_back.receive()
    by_block(bk, gkl, kg)
    spread(0)
    for exchange in (keys_fwd, values_fwd, values_back, keys_back):
        exchange.drain()
    for kv in range(2):
        head_wait(kv).wait_send()
    for store in stores:
        store.wait()
    gathered(1)
    gathered(0)


def land_kernel(a, b, c, d, ao, bo, co, do):
    ao[...] = a[...]
    bo[...] = b[...]
    co[...] = c[...]
    do[...] = d[...]


def land(*arrays):
    steps = 4
    specs = []
    for x in arrays:
        rows = x.shape[0] // steps
        specs.append(pl.BlockSpec((rows, x.shape[1]), lambda i: (i, 0)))
    return pl.pallas_call(
        land_kernel,
        grid=(steps,),
        in_specs=specs,
        out_specs=specs,
        out_shape=[jax.ShapeDtypeStruct(x.shape, x.dtype) for x in arrays],
        compiler_params=pltpu.CompilerParams(vmem_limit_bytes=60 << 20),
        name="land",
    )(*arrays)


def per_device(queries, key_states, value_states, block_lists, out_grad):
    bf16, f32, i32 = jnp.bfloat16, jnp.float32, jnp.int32
    wide, full = GROUP * HEAD_DIM, HEADS_AX * HEAD_DIM
    dma = pltpu.SemaphoreType.DMA
    vmem = pl.BlockSpec(memory_space=pltpu.VMEM)
    anywhere = pl.BlockSpec(memory_space=pl.ANY)

    def blocks(n, dtype):
        return pltpu.VMEM((n, BLK, HEAD_DIM), dtype)

    def bundles(rows):
        return pltpu.VMEM((rows, COLS, CAP, BLK, HEAD_DIM), bf16)

    exchange_sems = [
        dma((2, ROWS - 1)), dma((2, COLS)), dma((2, ROWS - 1, COLS - 1)), dma((2, ROWS - 1, 2)),
        dma((2, ROWS)), dma((2, COLS)),
    ]
    far = CTX * CAP
    att, dq, key_grad, value_grad = pl.pallas_call(
        mega_kernel,
        in_specs=[pl.BlockSpec(memory_space=pltpu.SMEM)] + [anywhere] * 4,
        out_specs=[anywhere, anywhere, vmem, vmem],
        out_shape=[
            jax.ShapeDtypeStruct((QB, BLK, wide), bf16),
            jax.ShapeDtypeStruct((QB, BLK, wide), bf16),
            jax.ShapeDtypeStruct((OWN, BLK, full), bf16),
            jax.ShapeDtypeStruct((OWN, BLK, full), bf16),
        ],
        scratch_shapes=[
            pltpu.VMEM((CTX, 1, 128), i32), pltpu.SMEM((CTX, 1, 128), i32),
            pltpu.VMEM((8, 128), i32), pltpu.SMEM((8, 128), i32),
            pltpu.VMEM((8, 128), i32), pltpu.SMEM((8, 128), i32),
            pltpu.VMEM((QB, BLK, wide), bf16), pltpu.VMEM((QB, BLK, wide), bf16),
            blocks(QB, bf16), blocks(QB, bf16), blocks(QB + far, bf16), blocks(QB + far, bf16),
            bundles(ROWS), bundles(ROWS),
            bundles(ROWS - 1), bundles(ROWS - 1), bundles(ROWS - 1), bundles(ROWS - 1),
            pltpu.VMEM((QB, LIST * BLK, GROUP * BLK), bf16),
            blocks(QB * LIST, f32), blocks(QB * LIST, f32),
            blocks(QB, f32), blocks(QB, f32), blocks(far, bf16), blocks(far, bf16),
            blocks(far, bf16), blocks(far, bf16), blocks(QB, bf16), blocks(QB, bf16),
        ]
        + [pltpu.VMEM((HEADS_AX, OWN, BLK, HEAD_DIM), bf16)] * 4
        + [pltpu.VMEM((QB, BLK, wide), bf16)] * 2
        + exchange_sems
        + exchange_sems
        + [
            dma((2,)), dma((2,)), dma((2,)), dma((2,)), dma((2,)), dma((2,)), dma((7,)), dma((2,)),
        ],
        compiler_params=pltpu.CompilerParams(
            collective_id=0, has_side_effects=True, vmem_limit_bytes=60 << 20
        ),
        name="mega",
    )(
        block_lists.T,
        key_states.reshape(OWN, BLK, full),
        value_states.reshape(OWN, BLK, full),
        queries.reshape(QB, BLK, wide),
        out_grad.reshape(QB, BLK, wide),
    )
    return land(
        att.reshape(TOK, wide),
        dq.reshape(TOK, wide),
        key_grad.reshape(OWN * BLK, full),
        value_grad.reshape(OWN * BLK, full),
    )


def solution(mesh):
    return jax.shard_map(
        per_device,
        mesh=mesh,
        in_specs=(
            P("ctx", "head"),
            P(("ctx", "head"), None),
            P(("ctx", "head"), None),
            P("ctx", None),
            P("ctx", "head"),
        ),
        out_specs=(
            P("ctx", "head"),
            P("ctx", "head"),
            P(("ctx", "head"), None),
            P(("ctx", "head"), None),
        ),
        check_vma=False,
    )
```
